256 devices in a mesh: down: 32 (over z_hi, y, core), cross: 8 (over z_lo, x).
Axes of the slice: x: 4, y: 4, z: 8 (z_hi: 4, z_lo: 2; z = z_hi * 2 + z_lo), core: 2. Of those that a mesh axis runs over, the one named last changes fastest.
Arguments:
- particles: float32 [32768, 12, 128], P(('down', 'cross')), may hold values from -4 to 14.5, as said below
- anchor_down: int32 [2, 32768], P(None, ('down', 'cross')), may hold values from -4 to 12
- anchor_cross: int32 [2, 32768], P(None, ('down', 'cross')), may hold values from -4 to 244
- move_count: int32 [2, 4, 32, 8], P(None, None, 'down', 'cross'), may hold values from 0 to 13, as said below
- move_slots: int32 [2, 4, 13, 32, 8], P(None, None, None, 'down', 'cross'), may hold values from 0 to 127, as said below
Outputs:
- moved_particles: float32 [32768, 12, 128], P(('down', 'cross'))
The draws below stay inside these ranges and needn't reach their ends.
Inputs may be any that keep to these rules, and one draw needn't show every extreme that they name: `move_count`: entry 0 of tile (i, j) equals entry 1 of tile (i + 1, j), and entry 2 of (i, j) equals entry 3 of (i, j + 1); entries toward the outside of the grid are 0; in every step some link carries 13. `move_slots`: for each step and tile the 52 slot numbers are different. `particles`: field 0 lies in [0.5, 8 - 1.5] and field 1 in [0.5, 16 - 1.5]; fields 7 to 10 are positive.
All inputs are finite; a program needn't handle non-finite values.
Results may differ from the reference program's by a relative error of at most 0.0003.
Values sent between devices are 32-bit elements; how exact they have to be, the bound alone decides.
A program may use at most 64 MiB of HBM per device.

```python
import math
import jax
import jax.numpy as jnp
from jax import lax

BLOCK_SIZE = 128
WIN_DOWN = 8
WIN_CROSS = 16
GHOST = 4
STEPS = 2
MOVE_CAP = 13
TILE_DOWN = 16
TILE_CROSS = 256
BLOCKS_DEV = 128
BLOCKS_ALL = 32768
NODES_DOWN = 512
NODES_CROSS = 2048
N_DOWN = 32
N_CROSS = 8


def draw_particles(key, part):
    key_list = jax.random.split(key, 11)
    grid_shape = (BLOCKS_ALL, BLOCK_SIZE)
    offset_down = jax.random.uniform(key_list[0], grid_shape, jnp.float32, 0.5, WIN_DOWN - 1.5)
    offset_cross = jax.random.uniform(key_list[1], grid_shape, jnp.float32, 0.5, WIN_CROSS - 1.5)
    speed_down = jnp.clip(jax.random.normal(key_list[2], grid_shape, jnp.float32), -4.0, 4.0)
    speed_cross = jnp.clip(jax.random.normal(key_list[3], grid_shape, jnp.float32), -4.0, 4.0)
    stress_all = jnp.clip(jax.random.normal(key_list[5], (BLOCKS_ALL, 3, BLOCK_SIZE), jnp.float32), -4.0, 4.0)
    mass_value = jnp.exp(jax.random.uniform(key_list[6], grid_shape, jnp.float32, math.log(0.5), math.log(2.0)))
    volume_value = jnp.exp(jax.random.uniform(key_list[7], grid_shape, jnp.float32, math.log(0.5), math.log(2.0)))
    shear_value = jnp.exp(jax.random.uniform(key_list[8], grid_shape, jnp.float32, 0.0, math.log(10.0)))
    lame_value = jnp.exp(jax.random.uniform(key_list[9], grid_shape, jnp.float32, 0.0, math.log(10.0)))
    strain_value = jax.random.uniform(key_list[10], grid_shape, jnp.float32, 0.0, 1.0)
    return jnp.stack([offset_down, offset_cross, speed_down, speed_cross, stress_all[:, 0], stress_all[:, 1], stress_all[:, 2], mass_value, volume_value, shear_value, lame_value, strain_value], axis=1)


def draw_move_count(key, part):
    key_list = jax.random.split(key, 4)
    links_down = jax.random.randint(key_list[0], (STEPS, N_DOWN - 1, N_CROSS), 0, MOVE_CAP + 1)
    links_cross = jax.random.randint(key_list[1], (STEPS, N_DOWN, N_CROSS - 1), 0, MOVE_CAP + 1)
    chosen_row = jax.random.randint(key_list[2], (STEPS, 1, 1), 0, N_DOWN - 1)
    chosen_col = jax.random.randint(key_list[3], (STEPS, 1, 1), 0, N_CROSS)
    row_index = jnp.arange(N_DOWN - 1)[None, :, None]
    col_index = jnp.arange(N_CROSS)[None, None, :]
    links_down = jnp.where((row_index == chosen_row) & (col_index == chosen_col), MOVE_CAP, links_down)
    forward_down = jnp.pad(links_down, ((0, 0), (0, 1), (0, 0)))
    backward_down = jnp.pad(links_down, ((0, 0), (1, 0), (0, 0)))
    forward_cross = jnp.pad(links_cross, ((0, 0), (0, 0), (0, 1)))
    backward_cross = jnp.pad(links_cross, ((0, 0), (0, 0), (1, 0)))
    return jnp.stack([forward_down, backward_down, forward_cross, backward_cross], axis=1).astype(jnp.int32)


def pick_slots(single_key):
    return jax.random.permutation(single_key, BLOCKS_DEV)[:4 * MOVE_CAP]


def draw_move_slots(key, part):
    key_list = jax.random.split(key, STEPS * N_DOWN * N_CROSS)
    picked = jax.vmap(pick_slots)(key_list)
    picked = picked.reshape(STEPS, N_DOWN, N_CROSS, 4, MOVE_CAP)
    return jnp.transpose(picked, (0, 3, 4, 1, 2)).astype(jnp.int32)


def with_ends(drawn, rng, smallest, high):
    spot = [jax.random.randint(jax.random.fold_in(rng, axis), (), 0, length) for axis, length in enumerate(drawn.shape)]
    longest = drawn.shape.index(max(drawn.shape))
    neighbour = spot[:longest] + [(spot[longest] + 1) % drawn.shape[longest]] + spot[longest + 1:]
    return drawn.at[tuple(spot)].set(smallest).at[tuple(neighbour)].set(high)


def setup_inputs(seed: int = 0) -> dict:
    streams_of = jax.random.split(jax.random.key(seed), 6)
    return {
        "particles": draw_particles(jax.random.fold_in(streams_of[5], 71), 0),
        "anchor_down": with_ends(jax.random.randint(streams_of[1], (STEPS, BLOCKS_ALL), -GHOST, TILE_DOWN + GHOST - WIN_DOWN + 1), jax.random.fold_in(streams_of[1], 1), -GHOST, TILE_DOWN + GHOST - WIN_DOWN).astype(jnp.int32),
        "anchor_cross": with_ends(jax.random.randint(streams_of[2], (STEPS, BLOCKS_ALL), -GHOST, TILE_CROSS + GHOST - WIN_CROSS + 1), jax.random.fold_in(streams_of[2], 1), -GHOST, TILE_CROSS + GHOST - WIN_CROSS).astype(jnp.int32),
        "move_count": draw_move_count(jax.random.fold_in(streams_of[5], 71), 0),
        "move_slots": draw_move_slots(jax.random.fold_in(streams_of[5], 71), 0),
    }


TIME_STEP = 0.1
GRAVITY = 5.6
MASS_FLOOR = 0.5
HIGHEST = lax.Precision.HIGHEST
group_limit = 256


def spline_pair(distance):
    magnitude = jnp.abs(distance)
    inside = 0.75 - distance * distance
    remote = 0.5 * (1.5 - magnitude) * (1.5 - magnitude)
    spline_value = jnp.where(magnitude < 0.5, inside, jnp.where(magnitude < 1.5, remote, 0.0))
    slope_far = jnp.where(distance > 0.0, distance - 1.5, distance + 1.5)
    spline_slope = jnp.where(magnitude < 0.5, -2.0 * distance, jnp.where(magnitude < 1.5, slope_far, 0.0))
    return spline_value, spline_slope


def block_weights(block_group):
    node_index = jnp.arange(WIN_DOWN * WIN_CROSS)
    node_row = (node_index // WIN_CROSS).astype(block_group.dtype)
    node_col = (node_index % WIN_CROSS).astype(block_group.dtype)
    down_value, down_slope = spline_pair(block_group[:, 0, :, None] - node_row)
    cross_value, cross_slope = spline_pair(block_group[:, 1, :, None] - node_col)
    return down_value * cross_value, down_slope * cross_value, down_value * cross_slope


def scatter_terms(block_group):
    weight, grad_down, grad_cross = block_weights(block_group)
    mass_value = block_group[:, 7]
    volume_value = block_group[:, 8]
    carried = jnp.stack([mass_value, mass_value * block_group[:, 2], mass_value * block_group[:, 3]], axis=1)
    stress_down = jnp.stack([-volume_value * block_group[:, 4], -volume_value * block_group[:, 5]], axis=1)
    stress_cross = jnp.stack([-volume_value * block_group[:, 5], -volume_value * block_group[:, 6]], axis=1)
    lumped = jnp.einsum("bcp,bpn->bcn", carried, weight, precision=HIGHEST)
    force_sum = jnp.einsum("bcp,bpn->bcn", stress_down, grad_down, precision=HIGHEST)
    force_sum = force_sum + jnp.einsum("bcp,bpn->bcn", stress_cross, grad_cross, precision=HIGHEST)
    return jnp.concatenate([lumped, force_sum], axis=1)


def advance(block_group, particle_vel, along_down, along_cross):
    rate_dd = along_down[:, 0]
    rate_cc = along_cross[:, 1]
    rate_dc = 0.5 * (along_cross[:, 0] + along_down[:, 1])
    trace_rate = rate_dd + rate_cc
    shear_value = block_group[:, 9]
    lame_value = block_group[:, 10]
    stress_dd = block_group[:, 4] + TIME_STEP * (lame_value * trace_rate + 2.0 * shear_value * rate_dd)
    stress_dc = block_group[:, 5] + TIME_STEP * (2.0 * shear_value * rate_dc)
    stress_cc = block_group[:, 6] + TIME_STEP * (lame_value * trace_rate + 2.0 * shear_value * rate_cc)
    offset_down = jnp.clip(block_group[:, 0] + TIME_STEP * particle_vel[:, 0], 0.5, WIN_DOWN - 1.5)
    offset_cross = jnp.clip(block_group[:, 1] + TIME_STEP * particle_vel[:, 1], 0.5, WIN_CROSS - 1.5)
    volume_value = block_group[:, 8] * (1.0 + TIME_STEP * trace_rate)
    strain_value = block_group[:, 11] + TIME_STEP * (rate_dd * rate_dd + rate_cc * rate_cc + 2.0 * rate_dc * rate_dc)
    return jnp.stack([offset_down, offset_cross, particle_vel[:, 0], particle_vel[:, 1], stress_dd, stress_dc, stress_cc, block_group[:, 7], volume_value, shear_value, lame_value, strain_value], axis=1)


def gather_terms(block_group, window_vel):
    weight, grad_down, grad_cross = block_weights(block_group)
    particle_vel = jnp.einsum("bcn,bpn->bcp", window_vel, weight, precision=HIGHEST)
    along_down = jnp.einsum("bcn,bpn->bcp", window_vel, grad_down, precision=HIGHEST)
    along_cross = jnp.einsum("bcn,bpn->bcp", window_vel, grad_cross, precision=HIGHEST)
    return advance(block_group, particle_vel, along_down, along_cross)


def by_groups(block_task, particle_state, *extra_args):
    block_count = particle_state.shape[0]
    group_size = math.gcd(block_count, group_limit)
    packed = tuple(member.reshape((block_count // group_size, group_size) + member.shape[1:]) for member in (particle_state,) + extra_args)

    def run_group(pieces):
        return block_task(*pieces)

    result = lax.map(run_group, packed)
    return result.reshape((block_count,) + result.shape[2:])


def node_velocity(node_sums, keep_mask):
    mass_sum = node_sums[0]
    moved_sum = jnp.stack([node_sums[1] + TIME_STEP * (node_sums[3] + GRAVITY * mass_sum), node_sums[2] + TIME_STEP * node_sums[4]])
    return jnp.where(keep_mask, moved_sum / jnp.maximum(mass_sum, MASS_FLOOR), 0.0)


def migrate(particle_state, slot_list, count_list):
    tile_down = jnp.arange(N_DOWN, dtype=jnp.int32)[:, None]
    tile_cross = jnp.arange(N_CROSS, dtype=jnp.int32)[None, :]
    shift_down = [1, -1, 0, 0]
    shift_cross = [0, 0, 1, -1]
    opposite = [1, 0, 3, 2]
    order_index = jnp.arange(BLOCKS_ALL, dtype=jnp.int32)
    for direction in range(4):
        near_down = jnp.clip(tile_down + shift_down[direction], 0, N_DOWN - 1)
        near_cross = jnp.clip(tile_cross + shift_cross[direction], 0, N_CROSS - 1)
        target_index = (tile_down * N_CROSS + tile_cross) * BLOCKS_DEV + slot_list[direction]
        source_index = (near_down * N_CROSS + near_cross) * BLOCKS_DEV + slot_list[opposite[direction]][:, near_down, near_cross]
        valid_mask = jnp.arange(MOVE_CAP, dtype=jnp.int32)[:, None, None] < count_list[direction][None]
        chosen = jnp.where(valid_mask, source_index, target_index).reshape(-1).astype(jnp.int32)
        order_index = order_index.at[target_index.reshape(-1).astype(jnp.int32)].set(chosen)
    return particle_state[order_index]


def reference(particles, anchor_down, anchor_cross, move_count, move_slots):
    particle_state = particles
    grid_width = NODES_CROSS + 2 * GHOST
    grid_height = NODES_DOWN + 2 * GHOST
    node_index = jnp.arange(WIN_DOWN * WIN_CROSS, dtype=jnp.int32)
    node_row = node_index // WIN_CROSS
    node_col = node_index % WIN_CROSS
    tile_index = jnp.arange(BLOCKS_ALL, dtype=jnp.int32) // BLOCKS_DEV
    tile_down = tile_index // N_CROSS
    tile_cross = tile_index % N_CROSS
    row_global = jnp.arange(NODES_DOWN, dtype=jnp.int32)
    col_global = jnp.arange(NODES_CROSS, dtype=jnp.int32)
    keep_rows = (row_global > 0) & (row_global < NODES_DOWN - 1)
    keep_cols = (col_global > 0) & (col_global < NODES_CROSS - 1)
    keep_mask = keep_rows[:, None] & keep_cols[None, :]
    for step_index in range(STEPS):
        first_row = tile_down * TILE_DOWN + anchor_down[step_index] + GHOST
        first_col = tile_cross * TILE_CROSS + anchor_cross[step_index] + GHOST
        flat_index = ((first_row[:, None] + node_row[None, :]) * grid_width + first_col[:, None] + node_col[None, :]).astype(jnp.int32)
        node_terms = by_groups(scatter_terms, particle_state)
        spread = jnp.transpose(node_terms, (1, 0, 2)).reshape(5, -1)
        node_sums = jnp.zeros((5, grid_height * grid_width), jnp.float32).at[:, flat_index.reshape(-1)].add(spread)
        node_sums = node_sums.reshape(5, grid_height, grid_width)[:, GHOST:GHOST + NODES_DOWN, GHOST:GHOST + NODES_CROSS]
        velocity_grid = node_velocity(node_sums, keep_mask)
        padded = jnp.pad(velocity_grid, ((0, 0), (GHOST, GHOST), (GHOST, GHOST))).reshape(2, -1)
        window_vel = jnp.transpose(padded[:, flat_index], (1, 0, 2))
        particle_state = by_groups(gather_terms, particle_state, window_vel)
        particle_state = migrate(particle_state, move_slots[step_index], move_count[step_index])
    return particle_state
```

```python
import jax
import jax.numpy as jnp
from jax import lax
from jax.experimental import pallas as pl
from jax.experimental.pallas import tpu as pltpu
from jax.sharding import PartitionSpec as P

WIN_DOWN = 8
WIN_CROSS = 16
GHOST = 4
STEPS = 2
MOVE_CAP = 13
TILE_DOWN = 16
TILE_CROSS = 256
BLOCKS = 128
FIELDS = 12
LANES = 128
TIME_STEP = 0.1
GRAVITY = 5.6
MASS_FLOOR = 0.5

F32 = jnp.float32
BF16 = jnp.bfloat16
MESH = pl.DeviceIdType.MESH

COLS = 272
BAND = 40
SPAN = 32
PAD = COLS - SPAN
CHUNK = 96
PITCH = 16
SLOTS = 16
OUT_ROWS = 4 * SLOTS * PITCH
ALL_ROWS = BLOCKS * PITCH
SEND_ROWS = MOVE_CAP * PITCH
STRIDE_PAD = 16
ORDER_0, ORDER_1, SOURCE_1, PLACE_1 = range(4)

NEAR = ((-1, 0), (1, 0), (0, -1), (0, 1), (-1, -1), (1, -1), (-1, 1), (1, 1))
MOVES = ((1, 0), (-1, 0), (0, 1), (0, -1))


def spline_pair(distance):
    magnitude = jnp.abs(distance)
    outer = jnp.maximum(1.5 - magnitude, 0.0)
    inner = jnp.maximum(0.5 - magnitude, 0.0)
    inner3 = 3.0 * inner
    value = 0.5 * (outer * outer - inner3 * inner)
    steep = outer - inner3
    return value, jnp.where(distance > 0.0, -steep, steep)


def split(x):
    high = x.astype(BF16)
    return high, (x - high.astype(F32)).astype(BF16)


def matmul_t(a, b):
    return lax.dot_general(a, b, (((1,), (1,)), ((), ())), preferred_element_type=F32)


def sum_rows(parts, sublane):
    half = []
    for k in range(4):
        a, b = parts[k], parts[k + 4]
        low = sublane < 4
        half.append(jnp.where(low, a, b) + pltpu.roll(jnp.where(low, b, a), 4, 0))
    quarter = []
    for k in range(2):
        a, b = half[k], half[k + 2]
        a = a + pltpu.roll(a, 6, 0)
        b = b + pltpu.roll(b, 2, 0)
        quarter.append(jnp.where(sublane % 4 < 2, a, b))
    a, b = quarter
    a = a + pltpu.roll(a, 7, 0)
    b = b + pltpu.roll(b, 1, 0)
    return jnp.where(sublane % 2 == 0, a, b)


def kernel(
    tables,
    anchor_down,
    anchor_cross,
    count,
    particles,
    result,
    stage,
    rows_kept,
    cols_kept,
    spread,
    grid,
    pack,
    row_in,
    col_in,
    window,
    leaving,
    arrived,
    state_1,
    state_2,
    halo_send,
    halo_recv,
    move_send,
    move_recv,
):
    flat_1 = state_1.reshape(ALL_ROWS + STRIDE_PAD, LANES)
    flat_2 = state_2.reshape(ALL_ROWS + STRIDE_PAD, LANES)
    size_down, size_cross = lax.axis_size("down"), lax.axis_size("cross")
    me_down, me_cross = lax.axis_index("down"), lax.axis_index("cross")

    def at(step):
        return (
            lax.rem(me_down + step[0] + size_down, size_down),
            lax.rem(me_cross + step[1] + size_cross, size_cross),
        )

    barrier = pltpu.get_barrier_semaphore()
    for step in NEAR:
        pl.semaphore_signal(barrier, inc=1, device_id=at(step), device_id_type=MESH)

    sublane = lax.broadcasted_iota(jnp.int32, (8, LANES), 0)
    lane8 = lax.broadcasted_iota(jnp.int32, (8, LANES), 1)
    row_number = lax.broadcasted_iota(jnp.int32, (24, LANES), 0).astype(F32)
    col_number = lax.broadcasted_iota(jnp.int32, (SPAN, LANES), 0).astype(F32)
    no_terms = jnp.zeros((BAND - 16, LANES), F32)
    no_tail = jnp.zeros((8, LANES), F32)

    for k in range(8):
        spread[k] = jnp.zeros(((PAD + SPAN + PAD) // 8, 8, LANES), F32)

    def strided(ref, first, field):
        return ref[pl.ds(first + field, 8, stride=PITCH), :]

    def slot_of(step, block):
        return block if step == 0 else tables[ORDER_0, block]

    def scatter(step, batch, fields):
        u, w, v_down, v_cross, s_dd, s_dc, s_cc, mass, volume = fields[:9]
        less = -volume
        values = [mass, mass * v_down, mass * v_cross, less * s_dd, less * s_dc, less * s_cc]
        bases = []
        for k in range(8):
            block = batch * 8 + k
            slot = slot_of(step, block)
            first_row = anchor_down[step, slot] + GHOST
            first_col = anchor_cross[step, slot] + GHOST
            group = lax.shift_right_logical(first_col, 4)
            bases.append(PAD // 8 - 2 * group)
            row_shift = first_row.astype(F32)
            col_shift = (first_col - 16 * group).astype(F32)
            r_value, r_slope = spline_pair(u[k : k + 1] - (row_number - row_shift))
            c_value, c_slope = spline_pair(w[k : k + 1] - (col_number - col_shift))
            c_high, c_low = split(c_value)
            d_high, d_low = split(c_slope)
            rows_kept[block] = jnp.concatenate([r_value, r_slope], axis=0)
            cols_kept[block, :, :LANES] = jnp.concatenate([c_high, c_low], axis=0)
            cols_kept[block, :, LANES:] = jnp.concatenate([d_high, d_low], axis=0)
            m, md, mc, dd, dc, cc = (x[k : k + 1] for x in values)
            first, second = [], []
            for g in range(3):
                r, s = r_value[8 * g : 8 * g + 8], r_slope[8 * g : 8 * g + 8]
                first += [r * m, r * md, r * mc, s * dd, s * dc]
                second += [no_terms, r * dc, r * cc]
            a_high, a_low = split(jnp.concatenate(first + [no_tail], axis=0))
            b_high, b_low = split(jnp.concatenate(second + [no_tail], axis=0))
            left = jnp.concatenate([c_high, c_low, c_high, d_high, d_low, d_high], axis=1)
            right = jnp.concatenate([a_high, a_high, a_low, b_high, b_high, b_low], axis=1)
            sums = matmul_t(left, right)
            for v in range(SPAN // 8):
                spread[k, PAD // 8 + v] = sums[8 * v : 8 * v + 8]
        for v in range(COLS // 8):
            total = grid[step, 8 * v : 8 * v + 8, :]
            for k in range(8):
                total = total + spread[k, bases[k] + v]
            grid[step, 8 * v : 8 * v + 8, :] = total

    def gather(step, batch, load_block, order, target, first):
        parts = [[] for _ in range(6)]
        for k in range(8):
            position = batch * 8 + k
            slot = tables[order, position]
            block = slot if step == 0 else tables[SOURCE_1, position]
            group = lax.shift_right_logical(anchor_cross[step, slot] + GHOST, 4)
            cols = cols_kept[block]
            moved = lax.dot_general(
                window[group],
                jnp.concatenate([cols, cols], axis=0),
                (((1,), (0,)), ((), ())),
                preferred_element_type=F32,
            )
            rows = rows_kept[block]
            sums = [None] * 6
            for g in range(3):
                r, s = rows[8 * g : 8 * g + 8], rows[24 + 8 * g : 32 + 8 * g]
                down, cross = moved[16 * g : 16 * g + 8], moved[16 * g + 8 : 16 * g + 16]
                terms = [
                    r * down[:, :LANES],
                    r * cross[:, :LANES],
                    s * down[:, :LANES],
                    s * cross[:, :LANES],
                    r * down[:, LANES:],
                    r * cross[:, LANES:],
                ]
                sums = [t if a is None else a + t for a, t in zip(sums, terms)]
            for held, total in zip(parts, sums):
                held.append(total)
            load_block(k, block)
        new_down, new_cross, l_dd, l_cd, l_dc, l_cc = (sum_rows(p, sublane) for p in parts)
        f = [strided(stage, 0, i) for i in range(FIELDS)]
        rate_dc = 0.5 * (l_dc + l_cd)
        trace = l_dd + l_cc
        shear, lame = f[9], f[10]
        updated = [
            jnp.clip(f[0] + TIME_STEP * new_down, 0.5, WIN_DOWN - 1.5),
            jnp.clip(f[1] + TIME_STEP * new_cross, 0.5, WIN_CROSS - 1.5),
            new_down,
            new_cross,
            f[4] + TIME_STEP * (lame * trace + 2.0 * shear * l_dd),
            f[5] + TIME_STEP * (2.0 * shear * rate_dc),
            f[6] + TIME_STEP * (lame * trace + 2.0 * shear * l_cc),
            f[7],
            f[8] * (1.0 + TIME_STEP * trace),
            shear,
            lame,
            f[11] + TIME_STEP * (l_dd * l_dd + l_cc * l_cc + 2.0 * rate_dc * rate_dc),
        ]
        for i, x in enumerate(updated):
            target[pl.ds(first + i, 8, stride=PITCH), :] = x

    def remote(source, target, send, recv, step):
        return pltpu.make_async_remote_copy(
            src_ref=source,
            dst_ref=target,
            send_sem=send,
            recv_sem=recv,
            device_id=at(step),
            device_id_type=MESH,
        )

    lane = lax.broadcasted_iota(jnp.int32, (CHUNK, LANES), 1)

    def placed(parts, shifts):
        out = [pltpu.roll(p, s, 1) if s else p for p, s in zip(parts, shifts)]
        where = lane[: out[0].shape[0]]
        if len(out) == 2:
            return jnp.where(where < BAND, out[0], out[1])
        return jnp.where(where < BAND, out[0], jnp.where(where < 2 * BAND, out[1], out[2]))

    def exchange(step):
        short = COLS - 2 * CHUNK
        a, b = grid[step, :CHUNK, :], grid[step, CHUNK : 2 * CHUNK, :]
        c = grid[step, 2 * CHUNK :, :]
        for side, shifts in enumerate(((0, 40, 80), (48, 88, 0))):
            pack[step, side, :short] = placed([a[:short], b[:short], c], shifts)
            pack[step, side, short:] = placed([a[short:], b[short:]], shifts[:2])
        first = grid.at[step, pl.ds(0, 8), :]
        last = grid.at[step, pl.ds(TILE_CROSS, 8), :]
        copies = []
        for n, (near, source, target) in enumerate(
            (
                ((-1, 0), pack.at[step, 0], row_in.at[step, 1]),
                ((1, 0), pack.at[step, 1], row_in.at[step, 0]),
                ((0, -1), first, col_in.at[step, 1]),
                ((0, 1), last, col_in.at[step, 0]),
                ((-1, -1), first, col_in.at[step, 5]),
                ((1, -1), first, col_in.at[step, 4]),
                ((-1, 1), last, col_in.at[step, 3]),
                ((1, 1), last, col_in.at[step, 2]),
            )
        ):
            copy = remote(source, target, halo_send.at[step, n], halo_recv.at[step, n], near)
            copy.start()
            copies.append(copy)
        return copies

    def velocities(step):
        above = me_down > 0
        below = me_down < size_down - 1
        before = me_cross > 0
        after = me_cross < size_cross - 1

        def keep(condition, mask, x):
            return jnp.where(mask & condition, x, 0.0)

        lane_1 = lane8
        low = lane_1 < BAND
        high = (lane_1 >= 2 * BAND) & (lane_1 < 3 * BAND)
        channel = lax.rem(lane_1, BAND) // 8
        row = 8 * (lane_1 // BAND) + lax.rem(lane_1, 8)
        row_global = me_down * TILE_DOWN - GHOST + row
        used = ((channel == 1) | (channel == 2)) & (lane_1 < 3 * BAND)
        row_keep = used & (row_global > 0) & (row_global < TILE_DOWN * size_down - 1)
        is_down = channel == 1
        pull = jnp.where(is_down, GRAVITY, 0.0)
        out = []
        for v in range(COLS // 8):
            total = grid[step, 8 * v : 8 * v + 8, :]
            part, inner = divmod(8 * v, CHUNK)
            from_above = row_in[step, 0, inner : inner + 8, :]
            from_below = row_in[step, 1, inner : inner + 8, :]
            turn = (LANES - BAND * part) % LANES
            total = total + keep(above, low, pltpu.roll(from_above, turn, 1) if turn else from_above)
            turn = (2 * BAND - BAND * part) % LANES
            total = total + keep(below, high, pltpu.roll(from_below, turn, 1) if turn else from_below)
            side = {0: (0, before, 2, 3), TILE_CROSS // 8: (1, after, 4, 5)}.get(v)
            if side:
                straight, there, up, down = side
                total = total + jnp.where(there, col_in[step, straight], 0.0)
                total = total + keep(there & above, low, pltpu.roll(col_in[step, up], 48, 1))
                total = total + keep(there & below, high, pltpu.roll(col_in[step, down], 80, 1))
            mass_down = pltpu.roll(total, 8, 1)
            mass = jnp.where(is_down, mass_down, pltpu.roll(total, 16, 1))
            force = pltpu.roll(total, LANES - 16, 1)
            moved = total + TIME_STEP * (force + pull * mass_down)
            col_global = me_cross * TILE_CROSS - GHOST + 8 * v + sublane
            inside = row_keep & (col_global > 0) & (col_global < TILE_CROSS * size_cross - 1)
            out.append(jnp.where(inside, moved / jnp.maximum(mass, MASS_FLOOR), 0.0))
        out += [no_tail] * (3 * LANES // 8 - len(out))
        turned = []
        for t in range(3):
            block = jnp.concatenate(out[16 * t : 16 * t + 16], axis=0).T
            turned.append(
                jnp.concatenate([block[BAND * g + 8 : BAND * g + 24] for g in range(3)], axis=0)
            )
        turned = jnp.concatenate(turned, axis=1)
        top = turned.astype(BF16).astype(F32)
        rest = turned - top
        for g in range(16):
            a, b = top[:, 16 * g : 16 * g + SPAN], rest[:, 16 * g : 16 * g + SPAN]
            window[g] = jnp.concatenate([a, a, b, b], axis=1).astype(BF16)

    def wait_all(copies):
        for copy in copies:
            copy.wait()

    def send_blocks(step):
        copies = []
        for k, near in enumerate(MOVES):
            copy = remote(
                leaving.at[step, pl.ds(k * SLOTS * PITCH, SEND_ROWS), :],
                arrived.at[step, pl.ds((k ^ 1) * SLOTS * PITCH, SEND_ROWS), :],
                move_send.at[step, k],
                move_recv.at[step, k],
                near,
            )
            copy.start()
            copies.append(copy)
        return copies

    for step in range(STEPS):
        grid[step] = jnp.zeros((COLS, LANES), F32)

    def scatter_0(batch, carry):
        for k in range(8):
            stage[PITCH * k : PITCH * k + FIELDS, :] = particles[batch * 8 + k]
        scatter(0, batch, [strided(stage, 0, i) for i in range(FIELDS)])
        return carry

    lax.fori_loop(0, BLOCKS // 8, scatter_0, 0)
    pl.semaphore_wait(barrier, len(NEAR))
    wait_all(exchange(0))
    velocities(0)

    def load_0(k, block):
        stage[PITCH * k : PITCH * k + FIELDS, :] = particles[block]

    def gather_leaving_0(batch, carry):
        gather(0, batch, load_0, ORDER_0, leaving.at[0], batch * 8 * PITCH)
        return carry

    def gather_staying_0(batch, carry):
        gather(0, batch, load_0, ORDER_0, flat_1, batch * 8 * PITCH)
        return carry

    lax.fori_loop(0, 8, gather_leaving_0, 0)
    copies = send_blocks(0)
    lax.fori_loop(8, 16, gather_staying_0, 0)

    def scatter_staying(batch, carry):
        scatter(1, batch, [strided(flat_1, batch * 8 * PITCH, i) for i in range(FIELDS)])
        return carry

    def scatter_arrived(batch, carry):
        first = batch * 8 * PITCH
        here = (lax.rem(batch, 2) * 8 + sublane) < count[0, batch // 2]
        fields = [
            jnp.where(here, strided(arrived.at[0], first, i), strided(leaving.at[0], first, i))
            for i in range(FIELDS)
        ]
        for i, x in enumerate(fields):
            flat_1[pl.ds(first + i, 8, stride=PITCH), :] = x
        scatter(1, batch, fields)
        return carry

    lax.fori_loop(8, 16, scatter_staying, 0)
    wait_all(copies)
    lax.fori_loop(0, 8, scatter_arrived, 0)
    wait_all(exchange(1))
    velocities(1)

    def load_1(k, block):
        stage[PITCH * k : PITCH * k + FIELDS, :] = state_1[block, :FIELDS, :]

    def gather_leaving_1(batch, carry):
        gather(1, batch, load_1, ORDER_1, leaving.at[1], batch * 8 * PITCH)
        return carry

    def gather_staying_1(batch, carry):
        gather(1, batch, load_1, ORDER_1, flat_2, batch * 8 * PITCH)
        return carry

    lax.fori_loop(0, 8, gather_leaving_1, 0)
    copies = send_blocks(1)
    lax.fori_loop(8, 16, gather_staying_1, 0)
    wait_all(copies)

    def settle(block, carry):
        here = jnp.full((PITCH, LANES), lax.rem(block, SLOTS)) < count[1, block // SLOTS]
        rows = pl.ds(pl.multiple_of(block * PITCH, PITCH), PITCH)
        state_2[block] = jnp.where(here, arrived[1, rows, :], leaving[1, rows, :])
        return carry

    lax.fori_loop(0, 4 * SLOTS, settle, 0, unroll=4)

    def put(slot, carry):
        place = tables[PLACE_1, slot]
        result[slot] = state_2[place, :FIELDS, :]
        return carry

    lax.fori_loop(0, BLOCKS, put, 0, unroll=4)


def slot_tables(move_slots):
    listed = jnp.pad(
        move_slots[:, :, :, 0, 0], ((0, 0), (0, 0), (0, SLOTS - MOVE_CAP)), constant_values=-1
    ).reshape(STEPS, 4 * SLOTS, 1)
    slot = jnp.arange(BLOCKS, dtype=jnp.int32)
    same = listed == slot
    position = jnp.arange(4 * SLOTS, dtype=jnp.int32)[:, None]
    used = jnp.sum(same.astype(jnp.int32), axis=1)
    there = jnp.sum(jnp.where(same, position, 0), axis=1)
    earlier = jnp.sum(((listed >= 0) & (listed < slot)).astype(jnp.int32), axis=1)
    rank = slot - earlier
    spare = 4 * (SLOTS - MOVE_CAP)
    third = rank // (SLOTS - MOVE_CAP)
    free = jnp.where(
        rank < spare,
        SLOTS * third + MOVE_CAP + rank - (SLOTS - MOVE_CAP) * third,
        4 * MOVE_CAP + rank,
    )
    place = jnp.where(used > 0, there, free)
    held = place[:, None, :] == slot[None, :, None]
    order = jnp.sum(jnp.where(held, slot, 0), axis=2)
    source = jnp.sum(jnp.where(held[1], place[0], 0), axis=1)
    return jnp.stack([order[0], order[1], source, place[1]])


def on_device(particles, anchor_down, anchor_cross, move_count, move_slots):
    smem = pl.BlockSpec(memory_space=pltpu.SMEM)
    vmem = pl.BlockSpec(memory_space=pltpu.VMEM)
    return pl.pallas_call(
        kernel,
        out_shape=jax.ShapeDtypeStruct(particles.shape, F32),
        in_specs=[smem, smem, smem, smem, vmem],
        out_specs=vmem,
        scratch_shapes=[
            pltpu.VMEM((8 * PITCH + STRIDE_PAD, LANES), F32),
            pltpu.VMEM((BLOCKS, 48, LANES), F32),
            pltpu.VMEM((BLOCKS, 2 * SPAN, 2 * LANES), BF16),
            pltpu.VMEM((8, (PAD + SPAN + PAD) // 8, 8, LANES), F32),
            pltpu.VMEM((STEPS, COLS, LANES), F32),
            pltpu.VMEM((STEPS, 2, CHUNK, LANES), F32),
            pltpu.VMEM((STEPS, 2, CHUNK, LANES), F32),
            pltpu.VMEM((STEPS, 6, 8, LANES), F32),
            pltpu.VMEM((16, 48, LANES), BF16),
            pltpu.VMEM((STEPS, OUT_ROWS + STRIDE_PAD, LANES), F32),
            pltpu.VMEM((STEPS, OUT_ROWS + STRIDE_PAD, LANES), F32),
            pltpu.VMEM((BLOCKS + 1, PITCH, LANES), F32),
            pltpu.VMEM((BLOCKS + 1, PITCH, LANES), F32),
            pltpu.SemaphoreType.DMA((STEPS, 8)),
            pltpu.SemaphoreType.DMA((STEPS, 8)),
            pltpu.SemaphoreType.DMA((STEPS, 4)),
            pltpu.SemaphoreType.DMA((STEPS, 4)),
        ],
        compiler_params=pltpu.CompilerParams(
            collective_id=0, has_side_effects=True, vmem_limit_bytes=40 * 1024 * 1024
        ),
    )(
        slot_tables(move_slots),
        anchor_down,
        anchor_cross,
        move_count[:, :, 0, 0],
        particles,
    )


def solution(mesh):
    return jax.shard_map(
        on_device,
        mesh=mesh,
        in_specs=(
            P(("down", "cross"), None, None),
            P(None, ("down", "cross")),
            P(None, ("down", "cross")),
            P(None, None, "down", "cross"),
            P(None, None, None, "down", "cross"),
        ),
        out_specs=P(("down", "cross"), None, None),
        check_vma=False,
    )
```

```python
import jax
import jax.numpy as jnp
from jax import lax
from jax.experimental import pallas as pl
from jax.experimental.pallas import tpu as pltpu
from jax.sharding import PartitionSpec as P

WIN_DOWN = 8
WIN_CROSS = 16
GHOST = 4
STEPS = 2
MOVE_CAP = 13
TILE_DOWN = 16
TILE_CROSS = 256
BLOCKS = 128
FIELDS = 12
LANES = 128
TIME_STEP = 0.1
GRAVITY = 5.6
MASS_FLOOR = 0.5

F32 = jnp.float32
BF16 = jnp.bfloat16
MESH = pl.DeviceIdType.MESH

COLS = 272
BAND = 40
SPAN = 32
PAD = COLS - SPAN
PITCH = 16
SLOTS = 16
OUT_ROWS = 4 * SLOTS * FIELDS
ALL_ROWS = BLOCKS * PITCH
SEND_ROWS = 8 * -(-MOVE_CAP * FIELDS // 8)
STRIDE_PAD = 16
LOADS = 4
ORDER_0, ORDER_1, SOURCE_1, PLACE_1 = range(4)

NEAR = ((-1, 0), (1, 0), (0, -1), (0, 1), (-1, -1), (1, -1), (-1, 1), (1, 1))
MOVES = ((1, 0), (-1, 0), (0, 1), (0, -1))


def spline_pair(distance):
    magnitude = jnp.abs(distance)
    outer = jnp.maximum(1.5 - magnitude, 0.0)
    inner = jnp.maximum(0.5 - magnitude, 0.0)
    inner3 = 3.0 * inner
    value = 0.5 * (outer * outer - inner3 * inner)
    steep = outer - inner3
    return value, jnp.where(distance > 0.0, -steep, steep)


def split(x):
    high = x.astype(BF16)
    return high, (x - high.astype(F32)).astype(BF16)


def matmul_t(a, b):
    return lax.dot_general(a, b, (((1,), (1,)), ((), ())), preferred_element_type=F32)


def sum_rows(parts, sublane):
    half = []
    for k in range(4):
        a, b = parts[k], parts[k + 4]
        low = sublane < 4
        half.append(jnp.where(low, a, b) + pltpu.roll(jnp.where(low, b, a), 4, 0))
    quarter = []
    for k in range(2):
        a, b = half[k], half[k + 2]
        a = a + pltpu.roll(a, 6, 0)
        b = b + pltpu.roll(b, 2, 0)
        quarter.append(jnp.where(sublane % 4 < 2, a, b))
    a, b = quarter
    a = a + pltpu.roll(a, 7, 0)
    b = b + pltpu.roll(b, 1, 0)
    return jnp.where(sublane % 2 == 0, a, b)


def kernel(
    tables,
    anchor_down,
    anchor_cross,
    count,
    fields_hbm,
    result,
    fields_in,
    stage,
    rows_kept,
    cols_kept,
    spread,
    grid,
    turned,
    band_in,
    col_in,
    window,
    leaving,
    arrived,
    state_0,
    state_1,
    state_2,
    halo_send,
    halo_recv,
    move_send,
    move_recv,
    load_sem,
):
    flat_0 = state_0.reshape(ALL_ROWS + STRIDE_PAD, LANES)
    flat_1 = state_1.reshape(ALL_ROWS + STRIDE_PAD, LANES)
    flat_2 = state_2.reshape(ALL_ROWS + STRIDE_PAD, LANES)
    size_down, size_cross = lax.axis_size("down"), lax.axis_size("cross")
    me_down, me_cross = lax.axis_index("down"), lax.axis_index("cross")

    def at(step):
        return (
            lax.rem(me_down + step[0] + size_down, size_down),
            lax.rem(me_cross + step[1] + size_cross, size_cross),
        )

    loads = []
    for n in range(LOADS):
        part = pl.ds(n * BLOCKS // LOADS, BLOCKS // LOADS)
        loads.append(
            pltpu.make_async_copy(
                fields_hbm.at[:, part, :], fields_in.at[:, part, :], load_sem.at[n]
            )
        )
        loads[n].start()

    barrier = pltpu.get_barrier_semaphore()
    for step in NEAR:
        pl.semaphore_signal(barrier, inc=1, device_id=at(step), device_id_type=MESH)

    sublane = lax.broadcasted_iota(jnp.int32, (8, LANES), 0)
    lane8 = lax.broadcasted_iota(jnp.int32, (8, LANES), 1)
    row_number = lax.broadcasted_iota(jnp.int32, (24, LANES), 0).astype(F32)
    col_number = lax.broadcasted_iota(jnp.int32, (SPAN, LANES), 0).astype(F32)
    no_terms = jnp.zeros((BAND - 16, LANES), F32)
    no_tail = jnp.zeros((8, LANES), F32)

    for k in range(8):
        spread[k] = jnp.zeros(((PAD + SPAN + PAD) // 8, 8, LANES), F32)

    def strided(ref, first, pitch):
        return [ref[pl.ds(first + i, 8, stride=pitch), :] for i in range(FIELDS)]

    def put_strided(ref, first, pitch, fields):
        for i, x in enumerate(fields):
            ref[pl.ds(first + i, 8, stride=pitch), :] = x

    def slot_of(step, block):
        return block if step == 0 else tables[ORDER_0, block]

    def scatter(step, batch, fields):
        u, w, v_down, v_cross, s_dd, s_dc, s_cc, mass, volume = fields[:9]
        less = -volume
        values = [mass, mass * v_down, mass * v_cross, less * s_dd, less * s_dc, less * s_cc]
        bases = []
        for k in range(8):
            block = batch * 8 + k
            slot = slot_of(step, block)
            first_row = anchor_down[step, slot] + GHOST
            first_col = anchor_cross[step, slot] + GHOST
            group = lax.shift_right_logical(first_col, 4)
            bases.append(PAD // 8 - 2 * group)
            row_shift = first_row.astype(F32)
            col_shift = (first_col - 16 * group).astype(F32)
            r_value, r_slope = spline_pair(u[k : k + 1] - (row_number - row_shift))
            c_value, c_slope = spline_pair(w[k : k + 1] - (col_number - col_shift))
            c_high, c_low = split(c_value)
            d_high, d_low = split(c_slope)
            rows_kept[block] = jnp.concatenate([r_value, r_slope], axis=0)
            cols_kept[block, :, :LANES] = jnp.concatenate([c_high, c_low], axis=0)
            cols_kept[block, :, LANES:] = jnp.concatenate([d_high, d_low], axis=0)
            m, md, mc, dd, dc, cc = (x[k : k + 1] for x in values)
            first, second = [], []
            for g in range(3):
                r, s = r_value[8 * g : 8 * g + 8], r_slope[8 * g : 8 * g + 8]
                first += [r * m, r * md, r * mc, s * dd, s * dc]
                second += [no_terms, r * dc, r * cc]
            a_high, a_low = split(jnp.concatenate(first + [no_tail], axis=0))
            b_high, b_low = split(jnp.concatenate(second + [no_tail], axis=0))
            left = jnp.concatenate([c_high, c_low, c_high, d_high, d_low, d_high], axis=1)
            a_high, a_low, b_high, b_low = a_high.T, a_low.T, b_high.T, b_low.T
            right = jnp.concatenate([a_high, a_high, a_low, b_high, b_high, b_low], axis=0)
            sums = jnp.dot(left, right, preferred_element_type=F32)
            for v in range(SPAN // 8):
                spread[k, PAD // 8 + v] = sums[8 * v : 8 * v + 8]
        held = [spread[k, pl.ds(bases[k], COLS // 8)] for k in range(8)]
        for v in range(COLS // 8):
            total = grid[step, 8 * v : 8 * v + 8, :]
            for part in held:
                total = total + part[v]
            grid[step, 8 * v : 8 * v + 8, :] = total

    def gather(step, batch, source, order, target, pitch):
        parts = [[] for _ in range(6)]
        for k in range(8):
            position = batch * 8 + k
            slot = tables[order, position]
            block = slot if step == 0 else tables[SOURCE_1, position]
            group = lax.shift_right_logical(anchor_cross[step, slot] + GHOST, 4)
            cols = cols_kept[block]
            moved = lax.dot_general(
                window[group],
                jnp.concatenate([cols, cols], axis=0),
                (((1,), (0,)), ((), ())),
                preferred_element_type=F32,
            )
            rows = rows_kept[block]
            sums = [None] * 6
            for g in range(3):
                r, s = rows[8 * g : 8 * g + 8], rows[24 + 8 * g : 32 + 8 * g]
                down, cross = moved[16 * g : 16 * g + 8], moved[16 * g + 8 : 16 * g + 16]
                terms = [
                    r * down[:, :LANES],
                    r * cross[:, :LANES],
                    s * down[:, :LANES],
                    s * cross[:, :LANES],
                    r * down[:, LANES:],
                    r * cross[:, LANES:],
                ]
                sums = [t if a is None else a + t for a, t in zip(sums, terms)]
            for held, total in zip(parts, sums):
                held.append(total)
            stage[PITCH * k : PITCH * k + PITCH, :] = source[block]
        new_down, new_cross, l_dd, l_cd, l_dc, l_cc = (sum_rows(p, sublane) for p in parts)
        f = strided(stage, 0, PITCH)
        rate_dc = 0.5 * (l_dc + l_cd)
        trace = l_dd + l_cc
        shear, lame = f[9], f[10]
        updated = [
            jnp.clip(f[0] + TIME_STEP * new_down, 0.5, WIN_DOWN - 1.5),
            jnp.clip(f[1] + TIME_STEP * new_cross, 0.5, WIN_CROSS - 1.5),
            new_down,
            new_cross,
            f[4] + TIME_STEP * (lame * trace + 2.0 * shear * l_dd),
            f[5] + TIME_STEP * (2.0 * shear * rate_dc),
            f[6] + TIME_STEP * (lame * trace + 2.0 * shear * l_cc),
            f[7],
            f[8] * (1.0 + TIME_STEP * trace),
            shear,
            lame,
            f[11] + TIME_STEP * (l_dd * l_dd + l_cc * l_cc + 2.0 * rate_dc * rate_dc),
        ]
        put_strided(target, batch * 8 * pitch, pitch, updated)

    def remote(source, target, send, recv, step):
        return pltpu.make_async_remote_copy(
            src_ref=source,
            dst_ref=target,
            send_sem=send,
            recv_sem=recv,
            device_id=at(step),
            device_id_type=MESH,
        )

    def exchange(step):
        first = grid.at[step, pl.ds(0, 8), :]
        last = grid.at[step, pl.ds(TILE_CROSS, 8), :]
        messages = [
            ((0, 1), last, col_in.at[step, 0]),
            ((0, -1), first, col_in.at[step, 1]),
            ((1, 1), last, col_in.at[step, 2]),
            ((-1, 1), last, col_in.at[step, 3]),
            ((1, -1), first, col_in.at[step, 4]),
            ((-1, -1), first, col_in.at[step, 5]),
            ((1, 0), last, col_in.at[step, 6]),
            ((-1, 0), last, col_in.at[step, 7]),
            ((1, 0), turned.at[step, pl.ds(2 * BAND, BAND), :], band_in.at[step, 0]),
            ((-1, 0), turned.at[step, pl.ds(0, BAND), :], band_in.at[step, 1]),
        ]
        copies = [
            remote(source, target, halo_send.at[step, n], halo_recv.at[step, n], near)
            for n, (near, source, target) in enumerate(messages)
        ]
        for copy in copies[:8]:
            copy.start()
        for t in range(2):
            side = slice(LANES * t, LANES * (t + 1))
            turned[step, :, side] = grid[step, side, :].T[: 3 * BAND]
        for copy in copies[8:]:
            copy.start()
        return copies

    def velocities(step):
        above = me_down > 0
        below = me_down < size_down - 1
        before = me_cross > 0
        after = me_cross < size_cross - 1
        low = lane8 < BAND
        high = (lane8 >= 2 * BAND) & (lane8 < 3 * BAND)
        few = lane8 < 8

        def from_above(there, n):
            return jnp.where(low & above & there, pltpu.roll(col_in[step, n], 48, 1), 0.0)

        def from_below(there, n):
            return jnp.where(high & below & there, pltpu.roll(col_in[step, n], 80, 1), 0.0)

        first = jnp.where(before, col_in[step, 0], 0.0) + from_above(before, 2) + from_below(before, 3)
        last = grid[step, TILE_CROSS : TILE_CROSS + 8, :] + jnp.where(after, col_in[step, 1], 0.0)
        last = last + from_above(after, 4) + from_below(after, 5)
        last = last + from_above(True, 6) + from_below(True, 7)
        edge = jnp.concatenate([first, last, jnp.zeros((LANES - 16, LANES), F32)], axis=0).T

        tiles = []
        for t in range(3):
            col_global = me_cross * TILE_CROSS - GHOST + LANES * t + lane8
            col_keep = (col_global > 0) & (col_global < TILE_CROSS * size_cross - 1)
            side = slice(LANES * t, LANES * (t + 1))
            found = []
            for g in range(3):
                row_global = me_down * TILE_DOWN - GHOST + 8 * g + sublane
                inside = col_keep & (row_global > 0) & (row_global < TILE_DOWN * size_down - 1)
                sums = []
                for channel in range(5):
                    here = slice(BAND * g + 8 * channel, BAND * g + 8 * channel + 8)
                    if t == 2:
                        sums.append(jnp.where(few, pltpu.roll(edge[here], LANES - 8, 1), 0.0))
                        continue
                    total = turned[step, here, side]
                    there = slice(8 * channel, 8 * channel + 8)
                    if g == 0:
                        total = total + jnp.where(above, band_in[step, 0, there, side], 0.0)
                    if g == 2:
                        total = total + jnp.where(below, band_in[step, 1, there, side], 0.0)
                    if t == 0:
                        total = total + jnp.where(few, edge[here], 0.0)
                    sums.append(total)
                mass, moved_down, moved_cross, force_down, force_cross = sums
                heavy = jnp.maximum(mass, MASS_FLOOR)
                v_down = (moved_down + TIME_STEP * (force_down + GRAVITY * mass)) / heavy
                v_cross = (moved_cross + TIME_STEP * force_cross) / heavy
                found += [jnp.where(inside, v_down, 0.0), jnp.where(inside, v_cross, 0.0)]
            tiles.append(jnp.concatenate(found, axis=0))
        tops = [x.astype(BF16).astype(F32) for x in tiles]
        rests = [x - top for x, top in zip(tiles, tops)]
        lane48 = lax.broadcasted_iota(jnp.int32, (48, LANES), 1)

        def turn(x, m):
            return pltpu.roll(x, 16 * m, 1) if m else x

        def side_by_side(a, b, c, d):
            return jnp.where(
                lane48 < 64,
                jnp.where(lane48 < 32, a, b),
                jnp.where(lane48 < 96, c, d),
            ).astype(BF16)

        for t in range(2):
            high_turned = [turn(tops[t], m) for m in range(8)]
            low_turned = [turn(rests[t], m) for m in range(8)]
            for q in range(7):
                window[8 * t + q] = side_by_side(
                    high_turned[(8 - q) % 8],
                    high_turned[(10 - q) % 8],
                    low_turned[(12 - q) % 8],
                    low_turned[(14 - q) % 8],
                )
            a = jnp.where(lane48 < 16, tops[t + 1], tops[t])
            b = jnp.where(lane48 < 16, rests[t + 1], rests[t])
            window[8 * t + 7] = side_by_side(turn(a, 1), turn(a, 3), turn(b, 5), turn(b, 7))

    def wait_all(copies):
        for copy in copies:
            copy.wait()

    def send_blocks(step):
        copies = []
        for k, near in enumerate(MOVES):
            copy = remote(
                leaving.at[step, pl.ds(k * SLOTS * FIELDS, SEND_ROWS), :],
                arrived.at[step, pl.ds((k ^ 1) * SLOTS * FIELDS, SEND_ROWS), :],
                move_send.at[step, k],
                move_recv.at[step, k],
                near,
            )
            copy.start()
            copies.append(copy)
        return copies

    for step in range(STEPS):
        grid[step] = jnp.zeros((COLS, LANES), F32)

    def scatter_0(batch, carry):
        rows = pl.ds(pl.multiple_of(batch * 8, 8), 8)
        fields = [fields_in[i, rows, :] for i in range(FIELDS)]
        put_strided(flat_0, batch * 8 * PITCH, PITCH, fields)
        scatter(0, batch, fields)
        return carry

    batches = BLOCKS // 8
    for n, load in enumerate(loads):
        load.wait()
        lax.fori_loop(n * batches // LOADS, (n + 1) * batches // LOADS, scatter_0, 0)
    pl.semaphore_wait(barrier, len(NEAR))
    wait_all(exchange(0))
    velocities(0)

    def gather_leaving_0(batch, carry):
        gather(0, batch, state_0, ORDER_0, leaving.at[0], FIELDS)
        return carry

    def gather_staying_0(batch, carry):
        gather(0, batch, state_0, ORDER_0, flat_1, PITCH)
        return carry

    lax.fori_loop(0, 8, gather_leaving_0, 0)
    copies = send_blocks(0)
    lax.fori_loop(8, 16, gather_staying_0, 0)

    def settled(step, batch):
        here = (lax.rem(batch, 2) * 8 + sublane) < count[step, batch // 2]
        first = batch * 8 * FIELDS
        came = strided(arrived.at[step], first, FIELDS)
        kept = strided(leaving.at[step], first, FIELDS)
        return [jnp.where(here, a, b) for a, b in zip(came, kept)]

    def scatter_staying(batch, carry):
        scatter(1, batch, strided(flat_1, batch * 8 * PITCH, PITCH))
        return carry

    def scatter_arrived(batch, carry):
        fields = settled(0, batch)
        put_strided(flat_1, batch * 8 * PITCH, PITCH, fields)
        scatter(1, batch, fields)
        return carry

    lax.fori_loop(8, 16, scatter_staying, 0)
    wait_all(copies)
    lax.fori_loop(0, 8, scatter_arrived, 0)
    wait_all(exchange(1))
    velocities(1)

    def gather_leaving_1(batch, carry):
        gather(1, batch, state_1, ORDER_1, leaving.at[1], FIELDS)
        return carry

    def gather_staying_1(batch, carry):
        gather(1, batch, state_1, ORDER_1, flat_2, PITCH)
        return carry

    lax.fori_loop(0, 8, gather_leaving_1, 0)
    copies = send_blocks(1)
    lax.fori_loop(8, 16, gather_staying_1, 0)
    wait_all(copies)

    def settle(batch, carry):
        put_strided(flat_2, batch * 8 * PITCH, PITCH, settled(1, batch))
        return carry

    lax.fori_loop(0, 8, settle, 0)

    def put(batch, carry):
        for k in range(8):
            place = tables[PLACE_1, batch * 8 + k]
            stage[PITCH * k : PITCH * k + PITCH, :] = state_2[place]
        rows = pl.ds(pl.multiple_of(batch * 8, 8), 8)
        for i, x in enumerate(strided(stage, 0, PITCH)):
            result[i, rows, :] = x
        return carry

    lax.fori_loop(0, BLOCKS // 8, put, 0)


def slot_tables(move_slots):
    listed = move_slots.reshape(STEPS, 4 * MOVE_CAP, 1)
    slot = jnp.arange(BLOCKS, dtype=jnp.int32)
    same = listed == slot
    number = jnp.arange(4 * MOVE_CAP, dtype=jnp.int32)[:, None]
    position = number + (SLOTS - MOVE_CAP) * (number // MOVE_CAP)
    used = jnp.sum(same.astype(jnp.int32), axis=1)
    there = jnp.sum(jnp.where(same, position, 0), axis=1)
    earlier = jnp.sum((listed < slot).astype(jnp.int32), axis=1)
    rank = slot - earlier
    spare = 4 * (SLOTS - MOVE_CAP)
    third = rank // (SLOTS - MOVE_CAP)
    free = jnp.where(
        rank < spare,
        SLOTS * third + MOVE_CAP + rank - (SLOTS - MOVE_CAP) * third,
        4 * MOVE_CAP + rank,
    )
    place = jnp.where(used > 0, there, free)
    held = place[:, None, :] == slot[None, :, None]
    order = jnp.sum(jnp.where(held, slot, 0), axis=2)
    source = jnp.sum(jnp.where(held[1], place[0], 0), axis=1)
    return jnp.stack([order[0], order[1], source, place[1]])


def on_device(particles, anchor_down, anchor_cross, move_count, move_slots):
    smem = pl.BlockSpec(memory_space=pltpu.SMEM)
    vmem = pl.BlockSpec(memory_space=pltpu.VMEM)
    by_field = pl.pallas_call(
        kernel,
        out_shape=jax.ShapeDtypeStruct((FIELDS, BLOCKS, LANES), F32),
        in_specs=[smem, smem, smem, smem, pl.BlockSpec(memory_space=pltpu.HBM)],
        out_specs=vmem,
        scratch_shapes=[
            pltpu.VMEM((FIELDS, BLOCKS, LANES), F32),
            pltpu.VMEM((8 * PITCH + STRIDE_PAD, LANES), F32),
            pltpu.VMEM((BLOCKS, 48, LANES), F32),
            pltpu.VMEM((BLOCKS, 2 * SPAN, 2 * LANES), BF16),
            pltpu.VMEM((8, (PAD + SPAN + PAD) // 8, 8, LANES), F32),
            pltpu.VMEM((STEPS, COLS, LANES), F32),
            pltpu.VMEM((STEPS, 3 * BAND, 2 * LANES), F32),
            pltpu.VMEM((STEPS, 2, BAND, 2 * LANES), F32),
            pltpu.VMEM((STEPS, 8, 8, LANES), F32),
            pltpu.VMEM((16, 48, LANES), BF16),
            pltpu.VMEM((STEPS, OUT_ROWS + STRIDE_PAD, LANES), F32),
            pltpu.VMEM((STEPS, OUT_ROWS + STRIDE_PAD, LANES), F32),
            pltpu.VMEM((BLOCKS + 1, PITCH, LANES), F32),
            pltpu.VMEM((BLOCKS + 1, PITCH, LANES), F32),
            pltpu.VMEM((BLOCKS + 1, PITCH, LANES), F32),
            pltpu.SemaphoreType.DMA((STEPS, 10)),
            pltpu.SemaphoreType.DMA((STEPS, 10)),
            pltpu.SemaphoreType.DMA((STEPS, 4)),
            pltpu.SemaphoreType.DMA((STEPS, 4)),
            pltpu.SemaphoreType.DMA((LOADS,)),
        ],
        compiler_params=pltpu.CompilerParams(
            collective_id=0, has_side_effects=True, vmem_limit_bytes=40 * 1024 * 1024
        ),
    )(
        slot_tables(move_slots),
        anchor_down,
        anchor_cross,
        move_count[:, :, 0, 0],
        jnp.transpose(particles, (1, 0, 2)),
    )
    return jnp.transpose(by_field, (1, 0, 2))


def solution(mesh):
    return jax.shard_map(
        on_device,
        mesh=mesh,
        in_specs=(
            P(("down", "cross"), None, None),
            P(None, ("down", "cross")),
            P(None, ("down", "cross")),
            P(None, None, "down", "cross"),
            P(None, None, None, "down", "cross"),
        ),
        out_specs=P(("down", "cross"), None, None),
        check_vma=False,
    )
```

```python
import jax
import jax.numpy as jnp
from jax import lax
from jax.experimental import pallas as pl
from jax.experimental.pallas import tpu as pltpu
from jax.sharding import PartitionSpec as P

WIN_DOWN = 8
WIN_CROSS = 16
GHOST = 4
STEPS = 2
MOVE_CAP = 13
TILE_DOWN = 16
TILE_CROSS = 256
BLOCKS = 128
FIELDS = 12
LANES = 128
TIME_STEP = 0.1
GRAVITY = 5.6
MASS_FLOOR = 0.5

F32 = jnp.float32
BF16 = jnp.bfloat16
MESH = pl.DeviceIdType.MESH

COLS = 272
BAND = 40
SPAN = 32
PAD = COLS - SPAN
PITCH = 16
SLOTS = 16
OUT_ROWS = 4 * SLOTS * FIELDS
ALL_ROWS = BLOCKS * PITCH
SEND_ROWS = 8 * -(-MOVE_CAP * FIELDS // 8)
STRIDE_PAD = 16
SCATTER_BATCHES = 4
GATHER_BATCHES = 4
LOADS = 4
ORDER_0, ORDER_1, SOURCE_1, PLACE_1 = range(4)

NEAR = ((-1, 0), (1, 0), (0, -1), (0, 1), (-1, -1), (1, -1), (-1, 1), (1, 1))
MOVES = ((1, 0), (-1, 0), (0, 1), (0, -1))


def spline_pair(distance):
    magnitude = jnp.abs(distance)
    outer = jnp.maximum(1.5 - magnitude, 0.0)
    inner = jnp.maximum(0.5 - magnitude, 0.0)
    inner3 = 3.0 * inner
    value = 0.5 * (outer * outer - inner3 * inner)
    steep = outer - inner3
    return value, jnp.where(distance > 0.0, -steep, steep)


def split(x):
    high = x.astype(BF16)
    return high, (x - high.astype(F32)).astype(BF16)


def matmul_t(a, b):
    return lax.dot_general(a, b, (((1,), (1,)), ((), ())), preferred_element_type=F32)


def sum_rows(parts, sublane):
    half = []
    for k in range(4):
        a, b = parts[k], parts[k + 4]
        low = sublane < 4
        half.append(jnp.where(low, a, b) + pltpu.roll(jnp.where(low, b, a), 4, 0))
    quarter = []
    for k in range(2):
        a, b = half[k], half[k + 2]
        a = a + pltpu.roll(a, 6, 0)
        b = b + pltpu.roll(b, 2, 0)
        quarter.append(jnp.where(sublane % 4 < 2, a, b))
    a, b = quarter
    a = a + pltpu.roll(a, 7, 0)
    b = b + pltpu.roll(b, 1, 0)
    return jnp.where(sublane % 2 == 0, a, b)


def kernel(
    tables,
    anchor_down,
    anchor_cross,
    count,
    fields_hbm,
    result,
    fields_in,
    stage,
    rows_kept,
    cols_kept,
    spread,
    grid,
    turned,
    band_in,
    col_in,
    window,
    leaving,
    arrived,
    state_0,
    state_1,
    state_2,
    halo_send,
    halo_recv,
    move_send,
    move_recv,
    load_sem,
):
    flat_0 = state_0.reshape(ALL_ROWS + STRIDE_PAD, LANES)
    flat_1 = state_1.reshape(ALL_ROWS + STRIDE_PAD, LANES)
    flat_2 = state_2.reshape(ALL_ROWS + STRIDE_PAD, LANES)
    size_down, size_cross = lax.axis_size("down"), lax.axis_size("cross")
    me_down, me_cross = lax.axis_index("down"), lax.axis_index("cross")

    def at(step):
        return (
            lax.rem(me_down + step[0] + size_down, size_down),
            lax.rem(me_cross + step[1] + size_cross, size_cross),
        )

    loads = []
    for n in range(LOADS):
        part = pl.ds(n * BLOCKS // LOADS, BLOCKS // LOADS)
        loads.append(
            pltpu.make_async_copy(
                fields_hbm.at[:, part, :], fields_in.at[:, part, :], load_sem.at[n]
            )
        )
        loads[n].start()

    barrier = pltpu.get_barrier_semaphore()
    for step in NEAR:
        pl.semaphore_signal(barrier, inc=1, device_id=at(step), device_id_type=MESH)

    sublane = lax.broadcasted_iota(jnp.int32, (8, LANES), 0)
    lane8 = lax.broadcasted_iota(jnp.int32, (8, LANES), 1)
    row_number = lax.broadcasted_iota(jnp.int32, (24, LANES), 0).astype(F32)
    col_number = lax.broadcasted_iota(jnp.int32, (SPAN, LANES), 0).astype(F32)
    no_terms = jnp.zeros((BAND - 16, LANES), F32)
    no_tail = jnp.zeros((8, LANES), F32)

    for k in range(8 * SCATTER_BATCHES):
        spread[k] = jnp.zeros(((PAD + SPAN + PAD) // 8, 8, LANES), F32)

    def strided(ref, first, pitch):
        return [ref[pl.ds(first + i, 8, stride=pitch), :] for i in range(FIELDS)]

    def put_strided(ref, first, pitch, fields):
        for i, x in enumerate(fields):
            ref[pl.ds(first + i, 8, stride=pitch), :] = x

    def slot_of(step, block):
        return block if step == 0 else tables[ORDER_0, block]

    def scatter_one(step, batch, fields, at_spread, bases):
        u, w, v_down, v_cross, s_dd, s_dc, s_cc, mass, volume = fields[:9]
        less = -volume
        values = [mass, mass * v_down, mass * v_cross, less * s_dd, less * s_dc, less * s_cc]
        for k in range(8):
            block = batch * 8 + k
            slot = slot_of(step, block)
            first_row = anchor_down[step, slot] + GHOST
            first_col = anchor_cross[step, slot] + GHOST
            group = lax.shift_right_logical(first_col, 4)
            bases.append(PAD // 8 - 2 * group)
            row_shift = first_row.astype(F32)
            col_shift = (first_col - 16 * group).astype(F32)
            r_value, r_slope = spline_pair(u[k : k + 1] - (row_number - row_shift))
            c_value, c_slope = spline_pair(w[k : k + 1] - (col_number - col_shift))
            c_high, c_low = split(c_value)
            d_high, d_low = split(c_slope)
            rows_kept[block] = jnp.concatenate([r_value, r_slope], axis=0)
            cols_kept[block, :, :LANES] = jnp.concatenate([c_high, c_low], axis=0)
            cols_kept[block, :, LANES:] = jnp.concatenate([d_high, d_low], axis=0)
            m, md, mc, dd, dc, cc = (x[k : k + 1] for x in values)
            first, second = [], []
            for g in range(3):
                r, s = r_value[8 * g : 8 * g + 8], r_slope[8 * g : 8 * g + 8]
                first += [r * m, r * md, r * mc, s * dd, s * dc]
                second += [no_terms, r * dc, r * cc]
            a_high, a_low = split(jnp.concatenate(first + [no_tail], axis=0))
            b_high, b_low = split(jnp.concatenate(second + [no_tail], axis=0))
            left = jnp.concatenate([c_high, c_low, c_high, d_high, d_low, d_high], axis=1)
            a_high, a_low, b_high, b_low = a_high.T, a_low.T, b_high.T, b_low.T
            right = jnp.concatenate([a_high, a_high, a_low, b_high, b_high, b_low], axis=0)
            sums = jnp.dot(left, right, preferred_element_type=F32)
            for v in range(SPAN // 8):
                spread[at_spread + k, PAD // 8 + v] = sums[8 * v : 8 * v + 8]

    def scatter(step, group, fields_of):
        bases = []
        for n in range(SCATTER_BATCHES):
            batch = group * SCATTER_BATCHES + n
            scatter_one(step, batch, fields_of(batch), 8 * n, bases)
        held = [spread[k, pl.ds(base, COLS // 8)] for k, base in enumerate(bases)]
        for v in range(COLS // 8):
            total = grid[step, 8 * v : 8 * v + 8, :]
            for part in held:
                total = total + part[v]
            grid[step, 8 * v : 8 * v + 8, :] = total

    def gather_one(step, batch, source, order, target, pitch, at_stage):
        parts = [[] for _ in range(6)]
        for k in range(8):
            position = batch * 8 + k
            slot = tables[order, position]
            block = slot if step == 0 else tables[SOURCE_1, position]
            group = lax.shift_right_logical(anchor_cross[step, slot] + GHOST, 4)
            cols = cols_kept[block]
            moved = lax.dot_general(
                window[group],
                jnp.concatenate([cols, cols], axis=0),
                (((1,), (0,)), ((), ())),
                preferred_element_type=F32,
            )
            rows = rows_kept[block]
            sums = [None] * 6
            for g in range(3):
                r, s = rows[8 * g : 8 * g + 8], rows[24 + 8 * g : 32 + 8 * g]
                down, cross = moved[16 * g : 16 * g + 8], moved[16 * g + 8 : 16 * g + 16]
                terms = [
                    r * down[:, :LANES],
                    r * cross[:, :LANES],
                    s * down[:, :LANES],
                    s * cross[:, :LANES],
                    r * down[:, LANES:],
                    r * cross[:, LANES:],
                ]
                sums = [t if a is None else a + t for a, t in zip(sums, terms)]
            for held, total in zip(parts, sums):
                held.append(total)
            stage[at_stage + PITCH * k : at_stage + PITCH * k + PITCH, :] = source[block]
        new_down, new_cross, l_dd, l_cd, l_dc, l_cc = (sum_rows(p, sublane) for p in parts)
        f = strided(stage, at_stage, PITCH)
        rate_dc = 0.5 * (l_dc + l_cd)
        trace = l_dd + l_cc
        shear, lame = f[9], f[10]
        updated = [
            jnp.clip(f[0] + TIME_STEP * new_down, 0.5, WIN_DOWN - 1.5),
            jnp.clip(f[1] + TIME_STEP * new_cross, 0.5, WIN_CROSS - 1.5),
            new_down,
            new_cross,
            f[4] + TIME_STEP * (lame * trace + 2.0 * shear * l_dd),
            f[5] + TIME_STEP * (2.0 * shear * rate_dc),
            f[6] + TIME_STEP * (lame * trace + 2.0 * shear * l_cc),
            f[7],
            f[8] * (1.0 + TIME_STEP * trace),
            shear,
            lame,
            f[11] + TIME_STEP * (l_dd * l_dd + l_cc * l_cc + 2.0 * rate_dc * rate_dc),
        ]
        put_strided(target, batch * 8 * pitch, pitch, updated)

    def gather(step, group, source, order, target, pitch):
        for n in range(GATHER_BATCHES):
            batch = group * GATHER_BATCHES + n
            gather_one(step, batch, source, order, target, pitch, 8 * PITCH * n)

    def remote(source, target, send, recv, step):
        return pltpu.make_async_remote_copy(
            src_ref=source,
            dst_ref=target,
            send_sem=send,
            recv_sem=recv,
            device_id=at(step),
            device_id_type=MESH,
        )

    def exchange(step):
        first = grid.at[step, pl.ds(0, 8), :]
        last = grid.at[step, pl.ds(TILE_CROSS, 8), :]
        messages = [
            ((1, 1), last, col_in.at[step, 2]),
            ((-1, 1), last, col_in.at[step, 3]),
            ((1, -1), first, col_in.at[step, 4]),
            ((-1, -1), first, col_in.at[step, 5]),
            ((1, 0), last, col_in.at[step, 6]),
            ((-1, 0), last, col_in.at[step, 7]),
            ((0, 1), last, col_in.at[step, 0]),
            ((0, -1), first, col_in.at[step, 1]),
            ((1, 0), turned.at[step, pl.ds(2 * BAND, BAND), :], band_in.at[step, 0]),
            ((-1, 0), turned.at[step, pl.ds(0, BAND), :], band_in.at[step, 1]),
        ]
        copies = [
            remote(source, target, halo_send.at[step, n], halo_recv.at[step, n], near)
            for n, (near, source, target) in enumerate(messages)
        ]
        for copy in copies[:8]:
            copy.start()
        for t in range(2):
            side = slice(LANES * t, LANES * (t + 1))
            turned[step, :, side] = grid[step, side, :].T[: 3 * BAND]
        for copy in copies[8:]:
            copy.start()
        return copies

    def velocities(step):
        above = me_down > 0
        below = me_down < size_down - 1
        before = me_cross > 0
        after = me_cross < size_cross - 1
        low = lane8 < BAND
        high = (lane8 >= 2 * BAND) & (lane8 < 3 * BAND)
        few = lane8 < 8

        def from_above(there, n):
            return jnp.where(low & above & there, pltpu.roll(col_in[step, n], 48, 1), 0.0)

        def from_below(there, n):
            return jnp.where(high & below & there, pltpu.roll(col_in[step, n], 80, 1), 0.0)

        first = jnp.where(before, col_in[step, 0], 0.0) + from_above(before, 2) + from_below(before, 3)
        last = grid[step, TILE_CROSS : TILE_CROSS + 8, :] + jnp.where(after, col_in[step, 1], 0.0)
        last = last + from_above(after, 4) + from_below(after, 5)
        last = last + from_above(True, 6) + from_below(True, 7)
        edge = jnp.concatenate([first, last, jnp.zeros((LANES - 16, LANES), F32)], axis=0).T

        tiles = []
        for t in range(3):
            col_global = me_cross * TILE_CROSS - GHOST + LANES * t + lane8
            col_keep = (col_global > 0) & (col_global < TILE_CROSS * size_cross - 1)
            side = slice(LANES * t, LANES * (t + 1))
            found = []
            for g in range(3):
                row_global = me_down * TILE_DOWN - GHOST + 8 * g + sublane
                inside = col_keep & (row_global > 0) & (row_global < TILE_DOWN * size_down - 1)
                sums = []
                for channel in range(5):
                    here = slice(BAND * g + 8 * channel, BAND * g + 8 * channel + 8)
                    if t == 2:
                        sums.append(jnp.where(few, pltpu.roll(edge[here], LANES - 8, 1), 0.0))
                        continue
                    total = turned[step, here, side]
                    there = slice(8 * channel, 8 * channel + 8)
                    if g == 0:
                        total = total + jnp.where(above, band_in[step, 0, there, side], 0.0)
                    if g == 2:
                        total = total + jnp.where(below, band_in[step, 1, there, side], 0.0)
                    if t == 0:
                        total = total + jnp.where(few, edge[here], 0.0)
                    sums.append(total)
                mass, moved_down, moved_cross, force_down, force_cross = sums
                heavy = jnp.maximum(mass, MASS_FLOOR)
                v_down = (moved_down + TIME_STEP * (force_down + GRAVITY * mass)) / heavy
                v_cross = (moved_cross + TIME_STEP * force_cross) / heavy
                found += [jnp.where(inside, v_down, 0.0), jnp.where(inside, v_cross, 0.0)]
            tiles.append(jnp.concatenate(found, axis=0))
        tops = [x.astype(BF16).astype(F32) for x in tiles]
        rests = [x - top for x, top in zip(tiles, tops)]
        lane48 = lax.broadcasted_iota(jnp.int32, (48, LANES), 1)

        def turn(x, m):
            return pltpu.roll(x, 16 * m, 1) if m else x

        def side_by_side(a, b, c, d):
            return jnp.where(
                lane48 < 64,
                jnp.where(lane48 < 32, a, b),
                jnp.where(lane48 < 96, c, d),
            ).astype(BF16)

        for t in range(2):
            high_turned = [turn(tops[t], m) for m in range(8)]
            low_turned = [turn(rests[t], m) for m in range(8)]
            for q in range(7):
                window[8 * t + q] = side_by_side(
                    high_turned[(8 - q) % 8],
                    high_turned[(10 - q) % 8],
                    low_turned[(12 - q) % 8],
                    low_turned[(14 - q) % 8],
                )
            a = jnp.where(lane48 < 16, tops[t + 1], tops[t])
            b = jnp.where(lane48 < 16, rests[t + 1], rests[t])
            window[8 * t + 7] = side_by_side(turn(a, 1), turn(a, 3), turn(b, 5), turn(b, 7))

    def wait_all(copies):
        for copy in copies:
            copy.wait()

    def send_blocks(step, first):
        copies = []
        for k in (first, first + 1):
            near = MOVES[k]
            copy = remote(
                leaving.at[step, pl.ds(k * SLOTS * FIELDS, SEND_ROWS), :],
                arrived.at[step, pl.ds((k ^ 1) * SLOTS * FIELDS, SEND_ROWS), :],
                move_send.at[step, k],
                move_recv.at[step, k],
                near,
            )
            copy.start()
            copies.append(copy)
        return copies

    for step in range(STEPS):
        grid[step] = jnp.zeros((COLS, LANES), F32)

    def fields_0(batch):
        rows = pl.ds(pl.multiple_of(batch * 8, 8), 8)
        fields = [fields_in[i, rows, :] for i in range(FIELDS)]
        put_strided(flat_0, batch * 8 * PITCH, PITCH, fields)
        return fields

    def scatter_0(group, carry):
        scatter(0, group, fields_0)
        return carry

    batches = BLOCKS // 8 // SCATTER_BATCHES
    for n, load in enumerate(loads):
        load.wait()
        lax.fori_loop(n * batches // LOADS, (n + 1) * batches // LOADS, scatter_0, 0)
    pl.semaphore_wait(barrier, len(NEAR))
    wait_all(exchange(0))
    velocities(0)

    def gather_leaving_0(batch, carry):
        gather(0, batch, state_0, ORDER_0, leaving.at[0], FIELDS)
        return carry

    def gather_staying_0(batch, carry):
        gather(0, batch, state_0, ORDER_0, flat_1, PITCH)
        return carry

    lax.fori_loop(0, 1, gather_leaving_0, 0)
    copies = send_blocks(0, 0)
    lax.fori_loop(1, 2, gather_leaving_0, 0)
    copies += send_blocks(0, 2)
    lax.fori_loop(2, 4, gather_staying_0, 0)

    def settled(step, batch):
        here = (lax.rem(batch, 2) * 8 + sublane) < count[step, batch // 2]
        first = batch * 8 * FIELDS
        came = strided(arrived.at[step], first, FIELDS)
        kept = strided(leaving.at[step], first, FIELDS)
        return [jnp.where(here, a, b) for a, b in zip(came, kept)]

    def fields_staying(batch):
        return strided(flat_1, batch * 8 * PITCH, PITCH)

    def fields_arrived(batch):
        fields = settled(0, batch)
        put_strided(flat_1, batch * 8 * PITCH, PITCH, fields)
        return fields

    def scatter_staying(group, carry):
        scatter(1, group, fields_staying)
        return carry

    def scatter_arrived(group, carry):
        scatter(1, group, fields_arrived)
        return carry

    lax.fori_loop(2, 4, scatter_staying, 0)
    wait_all(copies)
    lax.fori_loop(0, 2, scatter_arrived, 0)
    wait_all(exchange(1))
    velocities(1)

    def gather_leaving_1(batch, carry):
        gather(1, batch, state_1, ORDER_1, leaving.at[1], FIELDS)
        return carry

    def gather_staying_1(batch, carry):
        gather(1, batch, state_1, ORDER_1, flat_2, PITCH)
        return carry

    lax.fori_loop(0, 1, gather_leaving_1, 0)
    copies = send_blocks(1, 0)
    lax.fori_loop(1, 2, gather_leaving_1, 0)
    copies += send_blocks(1, 2)
    lax.fori_loop(2, 4, gather_staying_1, 0)
    wait_all(copies)

    def settle(batch, carry):
        put_strided(flat_2, batch * 8 * PITCH, PITCH, settled(1, batch))
        return carry

    lax.fori_loop(0, 8, settle, 0)

    def put(batch, carry):
        for k in range(8):
            place = tables[PLACE_1, batch * 8 + k]
            stage[PITCH * k : PITCH * k + PITCH, :] = state_2[place]
        rows = pl.ds(pl.multiple_of(batch * 8, 8), 8)
        for i, x in enumerate(strided(stage, 0, PITCH)):
            result[i, rows, :] = x
        return carry

    lax.fori_loop(0, BLOCKS // 8, put, 0)


def slot_tables(move_slots):
    listed = move_slots.reshape(STEPS, 4 * MOVE_CAP, 1)
    slot = jnp.arange(BLOCKS, dtype=jnp.int32)
    same = listed == slot
    number = jnp.arange(4 * MOVE_CAP, dtype=jnp.int32)[:, None]
    position = number + (SLOTS - MOVE_CAP) * (number // MOVE_CAP)
    used = jnp.sum(same.astype(jnp.int32), axis=1)
    there = jnp.sum(jnp.where(same, position, 0), axis=1)
    earlier = jnp.sum((listed < slot).astype(jnp.int32), axis=1)
    rank = slot - earlier
    spare = 4 * (SLOTS - MOVE_CAP)
    third = rank // (SLOTS - MOVE_CAP)
    free = jnp.where(
        rank < spare,
        SLOTS * third + MOVE_CAP + rank - (SLOTS - MOVE_CAP) * third,
        4 * MOVE_CAP + rank,
    )
    place = jnp.where(used > 0, there, free)
    held = place[:, None, :] == slot[None, :, None]
    order = jnp.sum(jnp.where(held, slot, 0), axis=2)
    source = jnp.sum(jnp.where(held[1], place[0], 0), axis=1)
    return jnp.stack([order[0], order[1], source, place[1]])


def on_device(particles, anchor_down, anchor_cross, move_count, move_slots):
    smem = pl.BlockSpec(memory_space=pltpu.SMEM)
    vmem = pl.BlockSpec(memory_space=pltpu.VMEM)
    by_field = pl.pallas_call(
        kernel,
        out_shape=jax.ShapeDtypeStruct((FIELDS, BLOCKS, LANES), F32),
        in_specs=[smem, smem, smem, smem, pl.BlockSpec(memory_space=pltpu.HBM)],
        out_specs=vmem,
        scratch_shapes=[
            pltpu.VMEM((FIELDS, BLOCKS, LANES), F32),
            pltpu.VMEM((8 * PITCH * GATHER_BATCHES + STRIDE_PAD, LANES), F32),
            pltpu.VMEM((BLOCKS, 48, LANES), F32),
            pltpu.VMEM((BLOCKS, 2 * SPAN, 2 * LANES), BF16),
            pltpu.VMEM((8 * SCATTER_BATCHES, (PAD + SPAN + PAD) // 8, 8, LANES), F32),
            pltpu.VMEM((STEPS, COLS, LANES), F32),
            pltpu.VMEM((STEPS, 3 * BAND, 2 * LANES), F32),
            pltpu.VMEM((STEPS, 2, BAND, 2 * LANES), F32),
            pltpu.VMEM((STEPS, 8, 8, LANES), F32),
            pltpu.VMEM((16, 48, LANES), BF16),
            pltpu.VMEM((STEPS, OUT_ROWS + STRIDE_PAD, LANES), F32),
            pltpu.VMEM((STEPS, OUT_ROWS + STRIDE_PAD, LANES), F32),
            pltpu.VMEM((BLOCKS + 1, PITCH, LANES), F32),
            pltpu.VMEM((BLOCKS + 1, PITCH, LANES), F32),
            pltpu.VMEM((BLOCKS + 1, PITCH, LANES), F32),
            pltpu.SemaphoreType.DMA((STEPS, 10)),
            pltpu.SemaphoreType.DMA((STEPS, 10)),
            pltpu.SemaphoreType.DMA((STEPS, 4)),
            pltpu.SemaphoreType.DMA((STEPS, 4)),
            pltpu.SemaphoreType.DMA((LOADS,)),
        ],
        compiler_params=pltpu.CompilerParams(
            collective_id=0, has_side_effects=True, vmem_limit_bytes=40 * 1024 * 1024
        ),
    )(
        slot_tables(move_slots),
        anchor_down,
        anchor_cross,
        move_count[:, :, 0, 0],
        jnp.transpose(particles, (1, 0, 2)),
    )
    return jnp.transpose(by_field, (1, 0, 2))


def solution(mesh):
    return jax.shard_map(
        on_device,
        mesh=mesh,
        in_specs=(
            P(("down", "cross"), None, None),
            P(None, ("down", "cross")),
            P(None, ("down", "cross")),
            P(None, None, "down", "cross"),
            P(None, None, None, "down", "cross"),
        ),
        out_specs=P(("down", "cross"), None, None),
        check_vma=False,
    )
```

```python
import jax
import jax.numpy as jnp
from jax import lax
from jax.experimental import pallas as pl
from jax.experimental.pallas import tpu as pltpu
from jax.sharding import PartitionSpec as P

WIN_DOWN = 8
WIN_CROSS = 16
GHOST = 4
STEPS = 2
MOVE_CAP = 13
TILE_DOWN = 16
TILE_CROSS = 256
BLOCKS = 128
FIELDS = 12
LANES = 128
TIME_STEP = 0.1
GRAVITY = 5.6
MASS_FLOOR = 0.5

F32 = jnp.float32
BF16 = jnp.bfloat16
MESH = pl.DeviceIdType.MESH

COLS = 272
BAND = 40
SPAN = 32
PAD = COLS - SPAN
PITCH = 16
SLOTS = 16
OUT_ROWS = 4 * SLOTS * FIELDS
ALL_ROWS = BLOCKS * PITCH
SEND_ROWS = 8 * -(-MOVE_CAP * FIELDS // 8)
STRIDE_PAD = 16
SCATTER_BATCHES = 4
GATHER_BATCHES = 4
LOADS = 4
ORDER_0, ORDER_1, SOURCE_1, PLACE_1 = range(4)

NEAR = ((-1, 0), (1, 0), (0, -1), (0, 1), (-1, -1), (1, -1), (-1, 1), (1, 1))
MOVES = ((1, 0), (-1, 0), (0, 1), (0, -1))


def spline_pair(distance):
    magnitude = jnp.abs(distance)
    outer = jnp.maximum(1.5 - magnitude, 0.0)
    inner = jnp.maximum(0.5 - magnitude, 0.0)
    inner3 = 3.0 * inner
    value = 0.5 * (outer * outer - inner3 * inner)
    steep = outer - inner3
    return value, jnp.where(distance > 0.0, -steep, steep)


def split(x):
    high = x.astype(BF16)
    return high, (x - high.astype(F32)).astype(BF16)


def matmul_t(a, b):
    return lax.dot_general(a, b, (((1,), (1,)), ((), ())), preferred_element_type=F32)


def sum_rows(parts, sublane):
    half = []
    for k in range(4):
        a, b = parts[k], parts[k + 4]
        low = sublane < 4
        half.append(jnp.where(low, a, b) + pltpu.roll(jnp.where(low, b, a), 4, 0))
    quarter = []
    for k in range(2):
        a, b = half[k], half[k + 2]
        a = a + pltpu.roll(a, 6, 0)
        b = b + pltpu.roll(b, 2, 0)
        quarter.append(jnp.where(sublane % 4 < 2, a, b))
    a, b = quarter
    a = a + pltpu.roll(a, 7, 0)
    b = b + pltpu.roll(b, 1, 0)
    return jnp.where(sublane % 2 == 0, a, b)


def kernel(
    move_slots_hbm,
    anchor_down_hbm,
    anchor_cross_hbm,
    count_hbm,
    fields_hbm,
    result,
    fields_in,
    stage,
    rows_kept,
    cols_kept,
    spread,
    grid,
    turned,
    band_in,
    col_in,
    window,
    leaving,
    arrived,
    state_0,
    state_1,
    state_2,
    halo_send,
    halo_recv,
    move_send,
    move_recv,
    load_sem,
    tables_made,
    tables,
    table_sem,
    move_slots,
    anchor_down,
    anchor_cross,
    count,
    small_sem,
):
    flat_0 = state_0.reshape(ALL_ROWS + STRIDE_PAD, LANES)
    flat_1 = state_1.reshape(ALL_ROWS + STRIDE_PAD, LANES)
    flat_2 = state_2.reshape(ALL_ROWS + STRIDE_PAD, LANES)
    size_down, size_cross = lax.axis_size("down"), lax.axis_size("cross")
    me_down, me_cross = lax.axis_index("down"), lax.axis_index("cross")

    def at(step):
        return (
            lax.rem(me_down + step[0] + size_down, size_down),
            lax.rem(me_cross + step[1] + size_cross, size_cross),
        )

    small = [
        pltpu.make_async_copy(source, target, small_sem.at[n])
        for n, (source, target) in enumerate(
            (
                (move_slots_hbm, move_slots),
                (anchor_down_hbm, anchor_down),
                (anchor_cross_hbm, anchor_cross),
                (count_hbm, count),
            )
        )
    ]
    for copy in small:
        copy.start()
    loads = []
    for n in range(LOADS):
        part = pl.ds(n * BLOCKS // LOADS, BLOCKS // LOADS)
        loads.append(
            pltpu.make_async_copy(
                fields_hbm.at[:, part, :], fields_in.at[:, part, :], load_sem.at[n]
            )
        )
        loads[n].start()

    barrier = pltpu.get_barrier_semaphore()
    for step in NEAR:
        pl.semaphore_signal(barrier, inc=1, device_id=at(step), device_id_type=MESH)

    sublane = lax.broadcasted_iota(jnp.int32, (8, LANES), 0)
    lane8 = lax.broadcasted_iota(jnp.int32, (8, LANES), 1)
    row_number = lax.broadcasted_iota(jnp.int32, (24, LANES), 0).astype(F32)
    col_number = lax.broadcasted_iota(jnp.int32, (SPAN, LANES), 0).astype(F32)
    no_terms = jnp.zeros((BAND - 16, LANES), F32)
    no_tail = jnp.zeros((8, LANES), F32)

    for k in range(8 * SCATTER_BATCHES):
        spread[k] = jnp.zeros(((PAD + SPAN + PAD) // 8, 8, LANES), F32)

    for copy in small:
        copy.wait()
    slot = lax.broadcasted_iota(jnp.int32, (1, LANES), 1)
    spare = SLOTS - MOVE_CAP
    places, held = [], []
    for step in range(STEPS):
        place = jnp.full((1, LANES), -1, jnp.int32)
        rank = slot
        for n in range(4 * MOVE_CAP):
            k, m = divmod(n, MOVE_CAP)
            listed = move_slots[4 * step + k, 0, m]
            place = jnp.where(slot == listed, SLOTS * k + m, place)
            rank = rank - jnp.where(slot > listed, 1, 0)
        group = sum(jnp.where(rank >= spare * n, 1, 0) for n in range(1, 4))
        free = jnp.where(
            rank < 4 * spare, (SLOTS - spare) * group + MOVE_CAP + rank, 4 * MOVE_CAP + rank
        )
        place = jnp.where(place < 0, free, place)
        position = lax.broadcasted_iota(jnp.int32, (BLOCKS, LANES), 0)
        held.append(jnp.where(position == place, 1.0, 0.0).astype(BF16))
        places.append(place)

    def by_position(values, n):
        rows = jnp.broadcast_to(values.astype(F32), (8, LANES)).astype(BF16)
        return matmul_t(rows, held[n]).astype(jnp.int32)

    row = lax.broadcasted_iota(jnp.int32, (8, LANES), 0)
    made = jnp.where(row == ORDER_0, by_position(slot, 0), places[1])
    made = jnp.where(row == ORDER_1, by_position(slot, 1), made)
    made = jnp.where(row == SOURCE_1, by_position(places[0], 1), made)
    tables_made[...] = jnp.clip(made, 0, BLOCKS - 1)
    tables_copy = pltpu.make_async_copy(tables_made, tables, table_sem)
    tables_copy.start()

    def strided(ref, first, pitch):
        return [ref[pl.ds(first + i, 8, stride=pitch), :] for i in range(FIELDS)]

    def put_strided(ref, first, pitch, fields):
        for i, x in enumerate(fields):
            ref[pl.ds(first + i, 8, stride=pitch), :] = x

    def slot_of(step, block):
        return block if step == 0 else tables[ORDER_0, block]

    def scatter_one(step, batch, fields, at_spread, bases):
        u, w, v_down, v_cross, s_dd, s_dc, s_cc, mass, volume = fields[:9]
        less = -volume
        values = [mass, mass * v_down, mass * v_cross, less * s_dd, less * s_dc, less * s_cc]
        for k in range(8):
            block = batch * 8 + k
            slot = slot_of(step, block)
            first_row = anchor_down[step, slot] + GHOST
            first_col = anchor_cross[step, slot] + GHOST
            group = lax.shift_right_logical(first_col, 4)
            bases.append(PAD // 8 - 2 * group)
            row_shift = first_row.astype(F32)
            col_shift = (first_col - 16 * group).astype(F32)
            r_value, r_slope = spline_pair(u[k : k + 1] - (row_number - row_shift))
            c_value, c_slope = spline_pair(w[k : k + 1] - (col_number - col_shift))
            c_high, c_low = split(c_value)
            d_high, d_low = split(c_slope)
            rows_kept[block] = jnp.concatenate([r_value, r_slope], axis=0)
            cols_kept[block, :, :LANES] = jnp.concatenate([c_high, c_low], axis=0)
            cols_kept[block, :, LANES:] = jnp.concatenate([d_high, d_low], axis=0)
            m, md, mc, dd, dc, cc = (x[k : k + 1] for x in values)
            first, second = [], []
            for g in range(3):
                r, s = r_value[8 * g : 8 * g + 8], r_slope[8 * g : 8 * g + 8]
                first += [r * m, r * md, r * mc, s * dd, s * dc]
                second += [no_terms, r * dc, r * cc]
            a_high, a_low = split(jnp.concatenate(first + [no_tail], axis=0))
            b_high, b_low = split(jnp.concatenate(second + [no_tail], axis=0))
            left = jnp.concatenate([c_high, c_low, c_high, d_high, d_low, d_high], axis=1)
            a_high, a_low, b_high, b_low = a_high.T, a_low.T, b_high.T, b_low.T
            right = jnp.concatenate([a_high, a_high, a_low, b_high, b_high, b_low], axis=0)
            sums = jnp.dot(left, right, preferred_element_type=F32)
            for v in range(SPAN // 8):
                spread[at_spread + k, PAD // 8 + v] = sums[8 * v : 8 * v + 8]

    def scatter(step, group, fields_of):
        bases = []
        for n in range(SCATTER_BATCHES):
            batch = group * SCATTER_BATCHES + n
            scatter_one(step, batch, fields_of(batch), 8 * n, bases)
        held = [spread[k, pl.ds(base, COLS // 8)] for k, base in enumerate(bases)]
        for v in range(COLS // 8):
            total = grid[step, 8 * v : 8 * v + 8, :]
            for part in held:
                total = total + part[v]
            grid[step, 8 * v : 8 * v + 8, :] = total

    def gather_one(step, batch, source, order, target, pitch, at_stage):
        parts = [[] for _ in range(6)]
        for k in range(8):
            position = batch * 8 + k
            slot = tables[order, position]
            block = slot if step == 0 else tables[SOURCE_1, position]
            group = lax.shift_right_logical(anchor_cross[step, slot] + GHOST, 4)
            cols = cols_kept[block]
            moved = lax.dot_general(
                window[group],
                jnp.concatenate([cols, cols], axis=0),
                (((1,), (0,)), ((), ())),
                preferred_element_type=F32,
            )
            rows = rows_kept[block]
            sums = [None] * 6
            for g in range(3):
                r, s = rows[8 * g : 8 * g + 8], rows[24 + 8 * g : 32 + 8 * g]
                down, cross = moved[16 * g : 16 * g + 8], moved[16 * g + 8 : 16 * g + 16]
                terms = [
                    r * down[:, :LANES],
                    r * cross[:, :LANES],
                    s * down[:, :LANES],
                    s * cross[:, :LANES],
                    r * down[:, LANES:],
                    r * cross[:, LANES:],
                ]
                sums = [t if a is None else a + t for a, t in zip(sums, terms)]
            for held, total in zip(parts, sums):
                held.append(total)
            stage[at_stage + PITCH * k : at_stage + PITCH * k + PITCH, :] = source[block]
        new_down, new_cross, l_dd, l_cd, l_dc, l_cc = (sum_rows(p, sublane) for p in parts)
        f = strided(stage, at_stage, PITCH)
        rate_dc = 0.5 * (l_dc + l_cd)
        trace = l_dd + l_cc
        shear, lame = f[9], f[10]
        updated = [
            jnp.clip(f[0] + TIME_STEP * new_down, 0.5, WIN_DOWN - 1.5),
            jnp.clip(f[1] + TIME_STEP * new_cross, 0.5, WIN_CROSS - 1.5),
            new_down,
            new_cross,
            f[4] + TIME_STEP * (lame * trace + 2.0 * shear * l_dd),
            f[5] + TIME_STEP * (2.0 * shear * rate_dc),
            f[6] + TIME_STEP * (lame * trace + 2.0 * shear * l_cc),
            f[7],
            f[8] * (1.0 + TIME_STEP * trace),
            shear,
            lame,
            f[11] + TIME_STEP * (l_dd * l_dd + l_cc * l_cc + 2.0 * rate_dc * rate_dc),
        ]
        put_strided(target, batch * 8 * pitch, pitch, updated)

    def gather(step, group, source, order, target, pitch):
        for n in range(GATHER_BATCHES):
            batch = group * GATHER_BATCHES + n
            gather_one(step, batch, source, order, target, pitch, 8 * PITCH * n)

    def remote(source, target, send, recv, step):
        return pltpu.make_async_remote_copy(
            src_ref=source,
            dst_ref=target,
            send_sem=send,
            recv_sem=recv,
            device_id=at(step),
            device_id_type=MESH,
        )

    def exchange(step):
        first = grid.at[step, pl.ds(0, 8), :]
        last = grid.at[step, pl.ds(TILE_CROSS, 8), :]
        messages = [
            ((1, 1), last, col_in.at[step, 2]),
            ((-1, 1), last, col_in.at[step, 3]),
            ((1, -1), first, col_in.at[step, 4]),
            ((-1, -1), first, col_in.at[step, 5]),
            ((1, 0), last, col_in.at[step, 6]),
            ((-1, 0), last, col_in.at[step, 7]),
            ((0, 1), last, col_in.at[step, 0]),
            ((0, -1), first, col_in.at[step, 1]),
            ((1, 0), turned.at[step, pl.ds(2 * BAND, BAND), :], band_in.at[step, 0]),
            ((-1, 0), turned.at[step, pl.ds(0, BAND), :], band_in.at[step, 1]),
        ]
        copies = [
            remote(source, target, halo_send.at[step, n], halo_recv.at[step, n], near)
            for n, (near, source, target) in enumerate(messages)
        ]
        for copy in copies[:8]:
            copy.start()
        for t in range(2):
            side = slice(LANES * t, LANES * (t + 1))
            turned[step, :, side] = grid[step, side, :].T[: 3 * BAND]
        for copy in copies[8:]:
            copy.start()
        return copies

    def velocities(step):
        above = me_down > 0
        below = me_down < size_down - 1
        before = me_cross > 0
        after = me_cross < size_cross - 1
        low = lane8 < BAND
        high = (lane8 >= 2 * BAND) & (lane8 < 3 * BAND)
        few = lane8 < 8

        def from_above(there, n):
            return jnp.where(low & above & there, pltpu.roll(col_in[step, n], 48, 1), 0.0)

        def from_below(there, n):
            return jnp.where(high & below & there, pltpu.roll(col_in[step, n], 80, 1), 0.0)

        first = jnp.where(before, col_in[step, 0], 0.0) + from_above(before, 2) + from_below(before, 3)
        last = grid[step, TILE_CROSS : TILE_CROSS + 8, :] + jnp.where(after, col_in[step, 1], 0.0)
        last = last + from_above(after, 4) + from_below(after, 5)
        last = last + from_above(True, 6) + from_below(True, 7)
        edge = jnp.concatenate([first, last, jnp.zeros((LANES - 16, LANES), F32)], axis=0).T

        tiles = []
        for t in range(3):
            col_global = me_cross * TILE_CROSS - GHOST + LANES * t + lane8
            col_keep = (col_global > 0) & (col_global < TILE_CROSS * size_cross - 1)
            side = slice(LANES * t, LANES * (t + 1))
            found = []
            for g in range(3):
                row_global = me_down * TILE_DOWN - GHOST + 8 * g + sublane
                inside = col_keep & (row_global > 0) & (row_global < TILE_DOWN * size_down - 1)
                sums = []
                for channel in range(5):
                    here = slice(BAND * g + 8 * channel, BAND * g + 8 * channel + 8)
                    if t == 2:
                        sums.append(jnp.where(few, pltpu.roll(edge[here], LANES - 8, 1), 0.0))
                        continue
                    total = turned[step, here, side]
                    there = slice(8 * channel, 8 * channel + 8)
                    if g == 0:
                        total = total + jnp.where(above, band_in[step, 0, there, side], 0.0)
                    if g == 2:
                        total = total + jnp.where(below, band_in[step, 1, there, side], 0.0)
                    if t == 0:
                        total = total + jnp.where(few, edge[here], 0.0)
                    sums.append(total)
                mass, moved_down, moved_cross, force_down, force_cross = sums
                heavy = jnp.maximum(mass, MASS_FLOOR)
                v_down = (moved_down + TIME_STEP * (force_down + GRAVITY * mass)) / heavy
                v_cross = (moved_cross + TIME_STEP * force_cross) / heavy
                found += [jnp.where(inside, v_down, 0.0), jnp.where(inside, v_cross, 0.0)]
            tiles.append(jnp.concatenate(found, axis=0))
        tops = [x.astype(BF16).astype(F32) for x in tiles]
        rests = [x - top for x, top in zip(tiles, tops)]
        lane48 = lax.broadcasted_iota(jnp.int32, (48, LANES), 1)

        def turn(x, m):
            return pltpu.roll(x, 16 * m, 1) if m else x

        def side_by_side(a, b, c, d):
            return jnp.where(
                lane48 < 64,
                jnp.where(lane48 < 32, a, b),
                jnp.where(lane48 < 96, c, d),
            ).astype(BF16)

        for t in range(2):
            high_turned = [turn(tops[t], m) for m in range(8)]
            low_turned = [turn(rests[t], m) for m in range(8)]
            for q in range(7):
                window[8 * t + q] = side_by_side(
                    high_turned[(8 - q) % 8],
                    high_turned[(10 - q) % 8],
                    low_turned[(12 - q) % 8],
                    low_turned[(14 - q) % 8],
                )
            a = jnp.where(lane48 < 16, tops[t + 1], tops[t])
            b = jnp.where(lane48 < 16, rests[t + 1], rests[t])
            window[8 * t + 7] = side_by_side(turn(a, 1), turn(a, 3), turn(b, 5), turn(b, 7))

    def wait_all(copies):
        for copy in copies:
            copy.wait()

    def send_blocks(step, first):
        copies = []
        for k in (first, first + 1):
            near = MOVES[k]
            copy = remote(
                leaving.at[step, pl.ds(k * SLOTS * FIELDS, SEND_ROWS), :],
                arrived.at[step, pl.ds((k ^ 1) * SLOTS * FIELDS, SEND_ROWS), :],
                move_send.at[step, k],
                move_recv.at[step, k],
                near,
            )
            copy.start()
            copies.append(copy)
        return copies

    for step in range(STEPS):
        grid[step] = jnp.zeros((COLS, LANES), F32)

    def fields_0(batch):
        rows = pl.ds(pl.multiple_of(batch * 8, 8), 8)
        fields = [fields_in[i, rows, :] for i in range(FIELDS)]
        put_strided(flat_0, batch * 8 * PITCH, PITCH, fields)
        return fields

    def scatter_0(group, carry):
        scatter(0, group, fields_0)
        return carry

    batches = BLOCKS // 8 // SCATTER_BATCHES
    for n, load in enumerate(loads):
        load.wait()
        lax.fori_loop(n * batches // LOADS, (n + 1) * batches // LOADS, scatter_0, 0)
    tables_copy.wait()
    pl.semaphore_wait(barrier, len(NEAR))
    wait_all(exchange(0))
    velocities(0)

    def gather_leaving_0(batch, carry):
        gather(0, batch, state_0, ORDER_0, leaving.at[0], FIELDS)
        return carry

    def gather_staying_0(batch, carry):
        gather(0, batch, state_0, ORDER_0, flat_1, PITCH)
        return carry

    lax.fori_loop(0, 1, gather_leaving_0, 0)
    copies = send_blocks(0, 0)
    lax.fori_loop(1, 2, gather_leaving_0, 0)
    copies += send_blocks(0, 2)
    lax.fori_loop(2, 4, gather_staying_0, 0)

    def settled(step, batch):
        here = (lax.rem(batch, 2) * 8 + sublane) < count[step, batch // 2]
        first = batch * 8 * FIELDS
        came = strided(arrived.at[step], first, FIELDS)
        kept = strided(leaving.at[step], first, FIELDS)
        return [jnp.where(here, a, b) for a, b in zip(came, kept)]

    def fields_staying(batch):
        return strided(flat_1, batch * 8 * PITCH, PITCH)

    def fields_arrived(batch):
        fields = settled(0, batch)
        put_strided(flat_1, batch * 8 * PITCH, PITCH, fields)
        return fields

    def scatter_staying(group, carry):
        scatter(1, group, fields_staying)
        return carry

    def scatter_arrived(group, carry):
        scatter(1, group, fields_arrived)
        return carry

    lax.fori_loop(2, 4, scatter_staying, 0)
    wait_all(copies)
    lax.fori_loop(0, 2, scatter_arrived, 0)
    wait_all(exchange(1))
    velocities(1)

    def gather_leaving_1(batch, carry):
        gather(1, batch, state_1, ORDER_1, leaving.at[1], FIELDS)
        return carry

    def gather_staying_1(batch, carry):
        gather(1, batch, state_1, ORDER_1, flat_2, PITCH)
        return carry

    lax.fori_loop(0, 1, gather_leaving_1, 0)
    copies = send_blocks(1, 0)
    lax.fori_loop(1, 2, gather_leaving_1, 0)
    copies += send_blocks(1, 2)
    lax.fori_loop(2, 4, gather_staying_1, 0)
    wait_all(copies)

    def settle(batch, carry):
        put_strided(flat_2, batch * 8 * PITCH, PITCH, settled(1, batch))
        return carry

    lax.fori_loop(0, 8, settle, 0)

    def put(batch, carry):
        for k in range(8):
            place = tables[PLACE_1, batch * 8 + k]
            stage[PITCH * k : PITCH * k + PITCH, :] = state_2[place]
        rows = pl.ds(pl.multiple_of(batch * 8, 8), 8)
        for i, x in enumerate(strided(stage, 0, PITCH)):
            result[i, rows, :] = x
        return carry

    lax.fori_loop(0, BLOCKS // 8, put, 0)


def on_device(particles, anchor_down, anchor_cross, move_count, move_slots):
    vmem = pl.BlockSpec(memory_space=pltpu.VMEM)
    by_field = pl.pallas_call(
        kernel,
        out_shape=jax.ShapeDtypeStruct((FIELDS, BLOCKS, LANES), F32),
        in_specs=[pl.BlockSpec(memory_space=pltpu.HBM)] * 5,
        out_specs=vmem,
        scratch_shapes=[
            pltpu.VMEM((FIELDS, BLOCKS, LANES), F32),
            pltpu.VMEM((8 * PITCH * GATHER_BATCHES + STRIDE_PAD, LANES), F32),
            pltpu.VMEM((BLOCKS, 48, LANES), F32),
            pltpu.VMEM((BLOCKS, 2 * SPAN, 2 * LANES), BF16),
            pltpu.VMEM((8 * SCATTER_BATCHES, (PAD + SPAN + PAD) // 8, 8, LANES), F32),
            pltpu.VMEM((STEPS, COLS, LANES), F32),
            pltpu.VMEM((STEPS, 3 * BAND, 2 * LANES), F32),
            pltpu.VMEM((STEPS, 2, BAND, 2 * LANES), F32),
            pltpu.VMEM((STEPS, 8, 8, LANES), F32),
            pltpu.VMEM((16, 48, LANES), BF16),
            pltpu.VMEM((STEPS, OUT_ROWS + STRIDE_PAD, LANES), F32),
            pltpu.VMEM((STEPS, OUT_ROWS + STRIDE_PAD, LANES), F32),
            pltpu.VMEM((BLOCKS + 1, PITCH, LANES), F32),
            pltpu.VMEM((BLOCKS + 1, PITCH, LANES), F32),
            pltpu.VMEM((BLOCKS + 1, PITCH, LANES), F32),
            pltpu.SemaphoreType.DMA((STEPS, 10)),
            pltpu.SemaphoreType.DMA((STEPS, 10)),
            pltpu.SemaphoreType.DMA((STEPS, 4)),
            pltpu.SemaphoreType.DMA((STEPS, 4)),
            pltpu.SemaphoreType.DMA((LOADS,)),
            pltpu.VMEM((8, LANES), jnp.int32),
            pltpu.SMEM((8, LANES), jnp.int32),
            pltpu.SemaphoreType.DMA,
            pltpu.SMEM((STEPS * 4, 1, MOVE_CAP), jnp.int32),
            pltpu.SMEM((STEPS, BLOCKS), jnp.int32),
            pltpu.SMEM((STEPS, BLOCKS), jnp.int32),
            pltpu.SMEM((STEPS, 4), jnp.int32),
            pltpu.SemaphoreType.DMA((4,)),
        ],
        compiler_params=pltpu.CompilerParams(
            collective_id=0, has_side_effects=True, vmem_limit_bytes=40 * 1024 * 1024
        ),
    )(
        *(
            pltpu.with_memory_space_constraint(x, pltpu.HBM)
            for x in (
                move_slots.reshape(STEPS * 4, 1, MOVE_CAP),
                anchor_down,
                anchor_cross,
                move_count[:, :, 0, 0],
                jnp.transpose(particles, (1, 0, 2)),
            )
        )
    )
    return jnp.transpose(by_field, (1, 0, 2))


def solution(mesh):
    return jax.shard_map(
        on_device,
        mesh=mesh,
        in_specs=(
            P(("down", "cross"), None, None),
            P(None, ("down", "cross")),
            P(None, ("down", "cross")),
            P(None, None, "down", "cross"),
            P(None, None, None, "down", "cross"),
        ),
        out_specs=P(("down", "cross"), None, None),
        check_vma=False,
    )
```

```python
import jax
import jax.numpy as jnp
from jax import lax
from jax.experimental import pallas as pl
from jax.experimental.pallas import tpu as pltpu
from jax.sharding import PartitionSpec as P

WIN_DOWN = 8
WIN_CROSS = 16
GHOST = 4
STEPS = 2
MOVE_CAP = 13
TILE_DOWN = 16
TILE_CROSS = 256
BLOCKS = 128
FIELDS = 12
LANES = 128
TIME_STEP = 0.1
GRAVITY = 5.6
MASS_FLOOR = 0.5

F32 = jnp.float32
BF16 = jnp.bfloat16
MESH = pl.DeviceIdType.MESH

COLS = 272
BAND = 40
SPAN = 32
PAD = COLS - SPAN
PITCH = 16
SLOTS = 16
OUT_ROWS = 4 * SLOTS * FIELDS
ALL_ROWS = BLOCKS * PITCH
SEND_ROWS = 8 * -(-MOVE_CAP * FIELDS // 8)
STRIDE_PAD = 16
SCATTER_BATCHES = 4
GATHER_BATCHES = 4
LOADS = 4
ORDER_0, ORDER_1, SOURCE_1, PLACE_1 = range(4)

NEAR = ((-1, 0), (1, 0), (0, -1), (0, 1), (-1, -1), (1, -1), (-1, 1), (1, 1))
MOVES = ((1, 0), (-1, 0), (0, 1), (0, -1))


def spline_pair(distance):
    magnitude = jnp.abs(distance)
    outer = jnp.maximum(1.5 - magnitude, 0.0)
    inner = jnp.maximum(0.5 - magnitude, 0.0)
    inner3 = 3.0 * inner
    value = 0.5 * (outer * outer - inner3 * inner)
    steep = outer - inner3
    return value, jnp.where(distance > 0.0, -steep, steep)


def split(x):
    high = x.astype(BF16)
    return high, (x - high.astype(F32)).astype(BF16)


def matmul_t(a, b):
    return lax.dot_general(a, b, (((1,), (1,)), ((), ())), preferred_element_type=F32)


def sum_rows(parts, sublane):
    half = []
    for k in range(4):
        a, b = parts[k], parts[k + 4]
        low = sublane < 4
        half.append(jnp.where(low, a, b) + pltpu.roll(jnp.where(low, b, a), 4, 0))
    quarter = []
    for k in range(2):
        a, b = half[k], half[k + 2]
        a = a + pltpu.roll(a, 6, 0)
        b = b + pltpu.roll(b, 2, 0)
        quarter.append(jnp.where(sublane % 4 < 2, a, b))
    a, b = quarter
    a = a + pltpu.roll(a, 7, 0)
    b = b + pltpu.roll(b, 1, 0)
    return jnp.where(sublane % 2 == 0, a, b)


def kernel(
    move_slots_hbm,
    anchor_down_hbm,
    anchor_cross_hbm,
    count_hbm,
    fields_hbm,
    result,
    fields_in,
    stage,
    rows_kept,
    cols_kept,
    spread,
    grid,
    turned,
    band_in,
    col_in,
    window,
    leaving,
    arrived,
    state_0,
    state_1,
    state_2,
    halo_send,
    halo_recv,
    move_send,
    move_recv,
    load_sem,
    tables_made,
    tables,
    table_sem,
    move_slots,
    anchor_down,
    anchor_cross,
    count,
    small_sem,
):
    flat_0 = state_0.reshape(ALL_ROWS + STRIDE_PAD, LANES)
    flat_1 = state_1.reshape(ALL_ROWS + STRIDE_PAD, LANES)
    flat_2 = state_2.reshape(ALL_ROWS + STRIDE_PAD, LANES)
    size_down, size_cross = lax.axis_size("down"), lax.axis_size("cross")
    me_down, me_cross = lax.axis_index("down"), lax.axis_index("cross")

    def at(step):
        return (
            lax.rem(me_down + step[0] + size_down, size_down),
            lax.rem(me_cross + step[1] + size_cross, size_cross),
        )

    small = [
        pltpu.make_async_copy(source, target, small_sem.at[n])
        for n, (source, target) in enumerate(
            (
                (move_slots_hbm, move_slots),
                (anchor_down_hbm, anchor_down),
                (anchor_cross_hbm, anchor_cross),
                (count_hbm, count),
            )
        )
    ]
    for copy in small:
        copy.start()
    loads = []
    for n in range(LOADS):
        part = pl.ds(n * BLOCKS // LOADS, BLOCKS // LOADS)
        loads.append(
            pltpu.make_async_copy(
                fields_hbm.at[:, part, :], fields_in.at[:, part, :], load_sem.at[n]
            )
        )
        loads[n].start()

    barrier = pltpu.get_barrier_semaphore()
    for step in NEAR:
        pl.semaphore_signal(barrier, inc=1, device_id=at(step), device_id_type=MESH)

    sublane = lax.broadcasted_iota(jnp.int32, (8, LANES), 0)
    lane8 = lax.broadcasted_iota(jnp.int32, (8, LANES), 1)
    row_number = lax.broadcasted_iota(jnp.int32, (24, LANES), 0).astype(F32)
    col_number = lax.broadcasted_iota(jnp.int32, (SPAN, LANES), 0).astype(F32)
    no_terms = jnp.zeros((BAND - 16, LANES), F32)
    no_tail = jnp.zeros((8, LANES), F32)

    for k in range(8 * SCATTER_BATCHES):
        spread[k] = jnp.zeros(((PAD + SPAN + PAD) // 8, 8, LANES), F32)

    for copy in small:
        copy.wait()
    slot = lax.broadcasted_iota(jnp.int32, (1, LANES), 1)
    spare = SLOTS - MOVE_CAP
    places, held = [], []
    for step in range(STEPS):
        place = jnp.full((1, LANES), -1, jnp.int32)
        rank = slot
        for n in range(4 * MOVE_CAP):
            k, m = divmod(n, MOVE_CAP)
            listed = move_slots[4 * step + k, 0, m]
            place = jnp.where(slot == listed, SLOTS * k + m, place)
            rank = rank - jnp.where(slot > listed, 1, 0)
        group = sum(jnp.where(rank >= spare * n, 1, 0) for n in range(1, 4))
        free = jnp.where(
            rank < 4 * spare, (SLOTS - spare) * group + MOVE_CAP + rank, 4 * MOVE_CAP + rank
        )
        place = jnp.where(place < 0, free, place)
        position = lax.broadcasted_iota(jnp.int32, (BLOCKS, LANES), 0)
        held.append(jnp.where(position == place, 1.0, 0.0).astype(BF16))
        places.append(place)

    def by_position(values, n):
        rows = jnp.broadcast_to(values.astype(F32), (8, LANES)).astype(BF16)
        return matmul_t(rows, held[n]).astype(jnp.int32)

    row = lax.broadcasted_iota(jnp.int32, (8, LANES), 0)
    made = jnp.where(row == ORDER_0, by_position(slot, 0), places[1])
    made = jnp.where(row == ORDER_1, by_position(slot, 1), made)
    made = jnp.where(row == SOURCE_1, by_position(places[0], 1), made)
    tables_made[...] = jnp.clip(made, 0, BLOCKS - 1)
    tables_copy = pltpu.make_async_copy(tables_made, tables, table_sem)
    tables_copy.start()

    def strided(ref, first, pitch):
        return [ref[pl.ds(first + i, 8, stride=pitch), :] for i in range(FIELDS)]

    def put_strided(ref, first, pitch, fields):
        for i, x in enumerate(fields):
            ref[pl.ds(first + i, 8, stride=pitch), :] = x

    def slot_of(step, block):
        return block if step == 0 else tables[ORDER_0, block]

    def scatter_one(step, batch, fields, at_spread, bases):
        u, w, v_down, v_cross, s_dd, s_dc, s_cc, mass, volume = fields[:9]
        less = -volume
        values = [mass, mass * v_down, mass * v_cross, less * s_dd, less * s_dc, less * s_cc]
        for k in range(8):
            block = batch * 8 + k
            slot = slot_of(step, block)
            first_row = anchor_down[step, slot] + GHOST
            first_col = anchor_cross[step, slot] + GHOST
            group = lax.shift_right_logical(first_col, 4)
            bases.append(PAD // 8 - 2 * group)
            row_shift = first_row.astype(F32)
            col_shift = (first_col - 16 * group).astype(F32)
            r_value, r_slope = spline_pair(u[k : k + 1] - (row_number - row_shift))
            c_value, c_slope = spline_pair(w[k : k + 1] - (col_number - col_shift))
            c_high, c_low = split(c_value)
            d_high, d_low = split(c_slope)
            rows_kept[block] = jnp.concatenate([r_value, r_slope], axis=0)
            cols_kept[block, :, :LANES] = jnp.concatenate([c_high, c_low], axis=0)
            cols_kept[block, :, LANES:] = jnp.concatenate([d_high, d_low], axis=0)
            m, md, mc, dd, dc, cc = (x[k : k + 1] for x in values)
            first, second = [], []
            for g in range(3):
                r, s = r_value[8 * g : 8 * g + 8], r_slope[8 * g : 8 * g + 8]
                first += [r * m, r * md, r * mc, s * dd, s * dc]
                second += [no_terms, r * dc, r * cc]
            a_high, a_low = split(jnp.concatenate(first + [no_tail], axis=0))
            b_high, b_low = split(jnp.concatenate(second + [no_tail], axis=0))
            left = jnp.concatenate([c_high, c_low, c_high, d_high, d_low, d_high], axis=1)
            a_high, a_low, b_high, b_low = a_high.T, a_low.T, b_high.T, b_low.T
            right = jnp.concatenate([a_high, a_high, a_low, b_high, b_high, b_low], axis=0)
            sums = jnp.dot(left, right, preferred_element_type=F32)
            for v in range(SPAN // 8):
                spread[at_spread + k, PAD // 8 + v] = sums[8 * v : 8 * v + 8]

    def scatter(step, group, fields_of):
        bases = []
        for n in range(SCATTER_BATCHES):
            batch = group * SCATTER_BATCHES + n
            scatter_one(step, batch, fields_of(batch), 8 * n, bases)
        held = [spread[k, pl.ds(base, COLS // 8)] for k, base in enumerate(bases)]
        for v in range(COLS // 8):
            total = grid[step, 8 * v : 8 * v + 8, :]
            for part in held:
                total = total + part[v]
            grid[step, 8 * v : 8 * v + 8, :] = total

    def gather_one(step, batch, source, order, target, pitch, at_stage):
        parts = [[] for _ in range(6)]
        for k in range(8):
            position = batch * 8 + k
            slot = tables[order, position]
            block = slot if step == 0 else tables[SOURCE_1, position]
            group = lax.shift_right_logical(anchor_cross[step, slot] + GHOST, 4)
            cols = cols_kept[block]
            moved = lax.dot_general(
                window[group],
                jnp.concatenate([cols, cols], axis=0),
                (((1,), (0,)), ((), ())),
                preferred_element_type=F32,
            )
            rows = rows_kept[block]
            sums = [None] * 6
            for g in range(3):
                r, s = rows[8 * g : 8 * g + 8], rows[24 + 8 * g : 32 + 8 * g]
                down, cross = moved[16 * g : 16 * g + 8], moved[16 * g + 8 : 16 * g + 16]
                terms = [
                    r * down[:, :LANES],
                    r * cross[:, :LANES],
                    s * down[:, :LANES],
                    s * cross[:, :LANES],
                    r * down[:, LANES:],
                    r * cross[:, LANES:],
                ]
                sums = [t if a is None else a + t for a, t in zip(sums, terms)]
            for held, total in zip(parts, sums):
                held.append(total)
            stage[at_stage + PITCH * k : at_stage + PITCH * k + PITCH, :] = source[block]
        new_down, new_cross, l_dd, l_cd, l_dc, l_cc = (sum_rows(p, sublane) for p in parts)
        f = strided(stage, at_stage, PITCH)
        rate_dc = 0.5 * (l_dc + l_cd)
        trace = l_dd + l_cc
        shear, lame = f[9], f[10]
        updated = [
            jnp.clip(f[0] + TIME_STEP * new_down, 0.5, WIN_DOWN - 1.5),
            jnp.clip(f[1] + TIME_STEP * new_cross, 0.5, WIN_CROSS - 1.5),
            new_down,
            new_cross,
            f[4] + TIME_STEP * (lame * trace + 2.0 * shear * l_dd),
            f[5] + TIME_STEP * (2.0 * shear * rate_dc),
            f[6] + TIME_STEP * (lame * trace + 2.0 * shear * l_cc),
            f[7],
            f[8] * (1.0 + TIME_STEP * trace),
            shear,
            lame,
            f[11] + TIME_STEP * (l_dd * l_dd + l_cc * l_cc + 2.0 * rate_dc * rate_dc),
        ]
        put_strided(target, batch * 8 * pitch, pitch, updated)

    def gather(step, group, source, order, target, pitch):
        for n in range(GATHER_BATCHES):
            batch = group * GATHER_BATCHES + n
            gather_one(step, batch, source, order, target, pitch, 8 * PITCH * n)

    def remote(source, target, send, recv, step):
        return pltpu.make_async_remote_copy(
            src_ref=source,
            dst_ref=target,
            send_sem=send,
            recv_sem=recv,
            device_id=at(step),
            device_id_type=MESH,
        )

    def exchange(step):
        first = grid.at[step, pl.ds(0, 8), :]
        last = grid.at[step, pl.ds(TILE_CROSS, 8), :]
        messages = [
            ((1, 1), last, col_in.at[step, 2]),
            ((-1, 1), last, col_in.at[step, 3]),
            ((1, -1), first, col_in.at[step, 4]),
            ((-1, -1), first, col_in.at[step, 5]),
            ((1, 0), last, col_in.at[step, 6]),
            ((-1, 0), last, col_in.at[step, 7]),
            ((0, 1), last, col_in.at[step, 0]),
            ((0, -1), first, col_in.at[step, 1]),
            ((1, 0), turned.at[step, pl.ds(2 * BAND, BAND), :], band_in.at[step, 0]),
            ((-1, 0), turned.at[step, pl.ds(0, BAND), :], band_in.at[step, 1]),
        ]
        copies = [
            remote(source, target, halo_send.at[step, n], halo_recv.at[step, n], near)
            for n, (near, source, target) in enumerate(messages)
        ]
        for copy in copies[:8]:
            copy.start()
        for t in range(2):
            side = slice(LANES * t, LANES * (t + 1))
            turned[step, :, side] = grid[step, side, :].T[: 3 * BAND]
        for copy in copies[8:]:
            copy.start()
        return copies

    def velocities(step):
        above = me_down > 0
        below = me_down < size_down - 1
        before = me_cross > 0
        after = me_cross < size_cross - 1
        low = lane8 < BAND
        high = (lane8 >= 2 * BAND) & (lane8 < 3 * BAND)
        few = lane8 < 8

        def from_above(there, n):
            return jnp.where(low & above & there, pltpu.roll(col_in[step, n], 48, 1), 0.0)

        def from_below(there, n):
            return jnp.where(high & below & there, pltpu.roll(col_in[step, n], 80, 1), 0.0)

        first = jnp.where(before, col_in[step, 0], 0.0) + from_above(before, 2) + from_below(before, 3)
        last = grid[step, TILE_CROSS : TILE_CROSS + 8, :] + jnp.where(after, col_in[step, 1], 0.0)
        last = last + from_above(after, 4) + from_below(after, 5)
        last = last + from_above(True, 6) + from_below(True, 7)
        edge = jnp.concatenate([first, last, jnp.zeros((LANES - 16, LANES), F32)], axis=0).T

        tiles = []
        for t in range(3):
            col_global = me_cross * TILE_CROSS - GHOST + LANES * t + lane8
            col_keep = (col_global > 0) & (col_global < TILE_CROSS * size_cross - 1)
            side = slice(LANES * t, LANES * (t + 1))
            found = []
            for g in range(3):
                row_global = me_down * TILE_DOWN - GHOST + 8 * g + sublane
                inside = col_keep & (row_global > 0) & (row_global < TILE_DOWN * size_down - 1)
                sums = []
                for channel in range(5):
                    here = slice(BAND * g + 8 * channel, BAND * g + 8 * channel + 8)
                    if t == 2:
                        sums.append(jnp.where(few, pltpu.roll(edge[here], LANES - 8, 1), 0.0))
                        continue
                    total = turned[step, here, side]
                    there = slice(8 * channel, 8 * channel + 8)
                    if g == 0:
                        total = total + jnp.where(above, band_in[step, 0, there, side], 0.0)
                    if g == 2:
                        total = total + jnp.where(below, band_in[step, 1, there, side], 0.0)
                    if t == 0:
                        total = total + jnp.where(few, edge[here], 0.0)
                    sums.append(total)
                mass, moved_down, moved_cross, force_down, force_cross = sums
                heavy = jnp.maximum(mass, MASS_FLOOR)
                v_down = (moved_down + TIME_STEP * (force_down + GRAVITY * mass)) / heavy
                v_cross = (moved_cross + TIME_STEP * force_cross) / heavy
                found += [jnp.where(inside, v_down, 0.0), jnp.where(inside, v_cross, 0.0)]
            tiles.append(jnp.concatenate(found, axis=0))
        tops = [x.astype(BF16).astype(F32) for x in tiles]
        rests = [x - top for x, top in zip(tiles, tops)]
        lane48 = lax.broadcasted_iota(jnp.int32, (48, LANES), 1)

        def turn(x, m):
            return pltpu.roll(x, 16 * m, 1) if m else x

        def side_by_side(a, b, c, d):
            return jnp.where(
                lane48 < 64,
                jnp.where(lane48 < 32, a, b),
                jnp.where(lane48 < 96, c, d),
            ).astype(BF16)

        for t in range(2):
            high_turned = [turn(tops[t], m) for m in range(8)]
            low_turned = [turn(rests[t], m) for m in range(8)]
            for q in range(7):
                window[8 * t + q] = side_by_side(
                    high_turned[(8 - q) % 8],
                    high_turned[(10 - q) % 8],
                    low_turned[(12 - q) % 8],
                    low_turned[(14 - q) % 8],
                )
            a = jnp.where(lane48 < 16, tops[t + 1], tops[t])
            b = jnp.where(lane48 < 16, rests[t + 1], rests[t])
            window[8 * t + 7] = side_by_side(turn(a, 1), turn(a, 3), turn(b, 5), turn(b, 7))

    def wait_all(copies):
        for copy in copies:
            copy.wait()

    def send_blocks(step, first):
        copies = []
        for k in (first, first + 1):
            near = MOVES[k]
            copy = remote(
                leaving.at[step, pl.ds(k * SLOTS * FIELDS, SEND_ROWS), :],
                arrived.at[step, pl.ds((k ^ 1) * SLOTS * FIELDS, SEND_ROWS), :],
                move_send.at[step, k],
                move_recv.at[step, k],
                near,
            )
            copy.start()
            copies.append(copy)
        return copies

    for step in range(STEPS):
        grid[step] = jnp.zeros((COLS, LANES), F32)

    def fields_0(batch):
        rows = pl.ds(pl.multiple_of(batch * 8, 8), 8)
        fields = [fields_in[i, rows, :] for i in range(FIELDS)]
        put_strided(flat_0, batch * 8 * PITCH, PITCH, fields)
        return fields

    def scatter_0(group, carry):
        scatter(0, group, fields_0)
        return carry

    batches = BLOCKS // 8 // SCATTER_BATCHES
    for n, load in enumerate(loads):
        load.wait()
        lax.fori_loop(n * batches // LOADS, (n + 1) * batches // LOADS, scatter_0, 0)
    tables_copy.wait()
    pl.semaphore_wait(barrier, len(NEAR))
    wait_all(exchange(0))
    velocities(0)

    def gather_leaving_0(batch, carry):
        gather(0, batch, state_0, ORDER_0, leaving.at[0], FIELDS)
        return carry

    def gather_staying_0(batch, carry):
        gather(0, batch, state_0, ORDER_0, flat_1, PITCH)
        return carry

    lax.fori_loop(0, 1, gather_leaving_0, 0)
    copies = send_blocks(0, 0)
    lax.fori_loop(1, 2, gather_leaving_0, 0)
    copies += send_blocks(0, 2)
    lax.fori_loop(2, 4, gather_staying_0, 0)

    def settled(step, batch):
        here = (lax.rem(batch, 2) * 8 + sublane) < count[step, batch // 2]
        first = batch * 8 * FIELDS
        came = strided(arrived.at[step], first, FIELDS)
        kept = strided(leaving.at[step], first, FIELDS)
        return [jnp.where(here, a, b) for a, b in zip(came, kept)]

    def fields_staying(batch):
        return strided(flat_1, batch * 8 * PITCH, PITCH)

    def fields_arrived(batch):
        fields = settled(0, batch)
        put_strided(flat_1, batch * 8 * PITCH, PITCH, fields)
        return fields

    def scatter_staying(group, carry):
        scatter(1, group, fields_staying)
        return carry

    def scatter_arrived(group, carry):
        scatter(1, group, fields_arrived)
        return carry

    lax.fori_loop(2, 4, scatter_staying, 0)
    wait_all(copies)
    lax.fori_loop(0, 2, scatter_arrived, 0)
    wait_all(exchange(1))
    velocities(1)

    def gather_leaving_1(batch, carry):
        gather(1, batch, state_1, ORDER_1, leaving.at[1], FIELDS)
        return carry

    def gather_staying_1(batch, carry):
        gather(1, batch, state_1, ORDER_1, flat_2, PITCH)
        return carry

    lax.fori_loop(0, 1, gather_leaving_1, 0)
    copies = send_blocks(1, 0)
    lax.fori_loop(1, 2, gather_leaving_1, 0)
    copies += send_blocks(1, 2)
    lax.fori_loop(2, 4, gather_staying_1, 0)
    wait_all(copies)

    def settle(group, carry):
        for n in range(4):
            batch = 4 * group + n
            put_strided(flat_2, batch * 8 * PITCH, PITCH, settled(1, batch))
        return carry

    lax.fori_loop(0, 2, settle, 0)

    def put(group, carry):
        for k in range(8 * GATHER_BATCHES):
            place = tables[PLACE_1, group * 8 * GATHER_BATCHES + k]
            stage[PITCH * k : PITCH * k + PITCH, :] = state_2[place]
        for n in range(GATHER_BATCHES):
            rows = pl.ds(pl.multiple_of((group * GATHER_BATCHES + n) * 8, 8), 8)
            for i, x in enumerate(strided(stage, 8 * PITCH * n, PITCH)):
                result[i, rows, :] = x
        return carry

    lax.fori_loop(0, BLOCKS // 8 // GATHER_BATCHES, put, 0)


def on_device(particles, anchor_down, anchor_cross, move_count, move_slots):
    vmem = pl.BlockSpec(memory_space=pltpu.VMEM)
    by_field = pl.pallas_call(
        kernel,
        out_shape=jax.ShapeDtypeStruct((FIELDS, BLOCKS, LANES), F32),
        in_specs=[pl.BlockSpec(memory_space=pltpu.HBM)] * 5,
        out_specs=vmem,
        scratch_shapes=[
            pltpu.VMEM((FIELDS, BLOCKS, LANES), F32),
            pltpu.VMEM((8 * PITCH * GATHER_BATCHES + STRIDE_PAD, LANES), F32),
            pltpu.VMEM((BLOCKS, 48, LANES), F32),
            pltpu.VMEM((BLOCKS, 2 * SPAN, 2 * LANES), BF16),
            pltpu.VMEM((8 * SCATTER_BATCHES, (PAD + SPAN + PAD) // 8, 8, LANES), F32),
            pltpu.VMEM((STEPS, COLS, LANES), F32),
            pltpu.VMEM((STEPS, 3 * BAND, 2 * LANES), F32),
            pltpu.VMEM((STEPS, 2, BAND, 2 * LANES), F32),
            pltpu.VMEM((STEPS, 8, 8, LANES), F32),
            pltpu.VMEM((16, 48, LANES), BF16),
            pltpu.VMEM((STEPS, OUT_ROWS + STRIDE_PAD, LANES), F32),
            pltpu.VMEM((STEPS, OUT_ROWS + STRIDE_PAD, LANES), F32),
            pltpu.VMEM((BLOCKS + 1, PITCH, LANES), F32),
            pltpu.VMEM((BLOCKS + 1, PITCH, LANES), F32),
            pltpu.VMEM((BLOCKS + 1, PITCH, LANES), F32),
            pltpu.SemaphoreType.DMA((STEPS, 10)),
            pltpu.SemaphoreType.DMA((STEPS, 10)),
            pltpu.SemaphoreType.DMA((STEPS, 4)),
            pltpu.SemaphoreType.DMA((STEPS, 4)),
            pltpu.SemaphoreType.DMA((LOADS,)),
            pltpu.VMEM((8, LANES), jnp.int32),
            pltpu.SMEM((8, LANES), jnp.int32),
            pltpu.SemaphoreType.DMA,
            pltpu.SMEM((STEPS * 4, 1, MOVE_CAP), jnp.int32),
            pltpu.SMEM((STEPS, BLOCKS), jnp.int32),
            pltpu.SMEM((STEPS, BLOCKS), jnp.int32),
            pltpu.SMEM((STEPS, 4), jnp.int32),
            pltpu.SemaphoreType.DMA((4,)),
        ],
        compiler_params=pltpu.CompilerParams(
            collective_id=0, has_side_effects=True, vmem_limit_bytes=40 * 1024 * 1024
        ),
    )(
        *(
            pltpu.with_memory_space_constraint(x, pltpu.HBM)
            for x in (
                move_slots.reshape(STEPS * 4, 1, MOVE_CAP),
                anchor_down,
                anchor_cross,
                move_count[:, :, 0, 0],
                jnp.transpose(particles, (1, 0, 2)),
            )
        )
    )
    return jnp.transpose(by_field, (1, 0, 2))


def solution(mesh):
    return jax.shard_map(
        on_device,
        mesh=mesh,
        in_specs=(
            P(("down", "cross"), None, None),
            P(None, ("down", "cross")),
            P(None, ("down", "cross")),
            P(None, None, "down", "cross"),
            P(None, None, None, "down", "cross"),
        ),
        out_specs=P(("down", "cross"), None, None),
        check_vma=False,
    )
```

```python
import jax
import jax.numpy as jnp
from jax import lax
from jax.experimental import pallas as pl
from jax.experimental.pallas import tpu as pltpu
from jax.sharding import PartitionSpec as P

WIN_DOWN = 8
WIN_CROSS = 16
GHOST = 4
STEPS = 2
MOVE_CAP = 13
TILE_DOWN = 16
TILE_CROSS = 256
BLOCKS = 128
FIELDS = 12
LANES = 128
TIME_STEP = 0.1
GRAVITY = 5.6
MASS_FLOOR = 0.5

F32 = jnp.float32
BF16 = jnp.bfloat16
MESH = pl.DeviceIdType.MESH

COLS = 272
BAND = 40
SPAN = 32
PAD = COLS - SPAN
PITCH = 16
SLOTS = 16
OUT_ROWS = 4 * SLOTS * FIELDS
ALL_ROWS = BLOCKS * PITCH
SEND_ROWS = 8 * -(-MOVE_CAP * FIELDS // 8)
STRIDE_PAD = 16
SCATTER_BATCHES = 4
GATHER_BATCHES = 4
LOADS = 2
ORDER_0, ORDER_1, SOURCE_1, PLACE_1 = range(4)

NEAR = ((-1, 0), (1, 0), (0, -1), (0, 1), (-1, -1), (1, -1), (-1, 1), (1, 1))
MOVES = ((1, 0), (-1, 0), (0, 1), (0, -1))


def spline_pair(distance):
    magnitude = jnp.abs(distance)
    outer = jnp.maximum(1.5 - magnitude, 0.0)
    inner = jnp.maximum(0.5 - magnitude, 0.0)
    inner3 = 3.0 * inner
    value = 0.5 * (outer * outer - inner3 * inner)
    steep = outer - inner3
    return value, jnp.where(distance > 0.0, -steep, steep)


def split(x):
    high = x.astype(BF16)
    return high, (x - high.astype(F32)).astype(BF16)


def matmul_t(a, b):
    return lax.dot_general(a, b, (((1,), (1,)), ((), ())), preferred_element_type=F32)


def sum_rows(parts, sublane):
    half = []
    for k in range(4):
        a, b = parts[k], parts[k + 4]
        low = sublane < 4
        half.append(jnp.where(low, a, b) + pltpu.roll(jnp.where(low, b, a), 4, 0))
    quarter = []
    for k in range(2):
        a, b = half[k], half[k + 2]
        a = a + pltpu.roll(a, 6, 0)
        b = b + pltpu.roll(b, 2, 0)
        quarter.append(jnp.where(sublane % 4 < 2, a, b))
    a, b = quarter
    a = a + pltpu.roll(a, 7, 0)
    b = b + pltpu.roll(b, 1, 0)
    return jnp.where(sublane % 2 == 0, a, b)


def kernel(
    move_slots_hbm,
    anchor_down_hbm,
    anchor_cross_hbm,
    count_hbm,
    fields_hbm,
    result,
    fields_in,
    stage,
    rows_kept,
    cols_kept,
    spread,
    grid,
    turned,
    band_in,
    col_in,
    window,
    leaving,
    arrived,
    state_0,
    state_1,
    state_2,
    halo_send,
    halo_recv,
    move_send,
    move_recv,
    load_sem,
    tables_made,
    tables,
    table_sem,
    move_slots,
    anchor_down,
    anchor_cross,
    count,
    small_sem,
):
    flat_0 = state_0.reshape(ALL_ROWS + STRIDE_PAD, LANES)
    flat_1 = state_1.reshape(ALL_ROWS + STRIDE_PAD, LANES)
    flat_2 = state_2.reshape(ALL_ROWS + STRIDE_PAD, LANES)
    size_down, size_cross = lax.axis_size("down"), lax.axis_size("cross")
    me_down, me_cross = lax.axis_index("down"), lax.axis_index("cross")

    def at(step):
        return (
            lax.rem(me_down + step[0] + size_down, size_down),
            lax.rem(me_cross + step[1] + size_cross, size_cross),
        )

    small = [
        pltpu.make_async_copy(source, target, small_sem.at[n])
        for n, (source, target) in enumerate(
            (
                (move_slots_hbm, move_slots),
                (anchor_down_hbm, anchor_down),
                (anchor_cross_hbm, anchor_cross),
                (count_hbm, count),
            )
        )
    ]
    for copy in small:
        copy.start()
    loads = []
    for n in range(LOADS):
        part = pl.ds(n * BLOCKS // LOADS, BLOCKS // LOADS)
        loads.append(
            pltpu.make_async_copy(
                fields_hbm.at[:, part, :], fields_in.at[:, part, :], load_sem.at[n]
            )
        )
        loads[n].start()

    barrier = pltpu.get_barrier_semaphore()
    for step in NEAR:
        pl.semaphore_signal(barrier, inc=1, device_id=at(step), device_id_type=MESH)

    sublane = lax.broadcasted_iota(jnp.int32, (8, LANES), 0)
    lane8 = lax.broadcasted_iota(jnp.int32, (8, LANES), 1)
    row_number = lax.broadcasted_iota(jnp.int32, (24, LANES), 0).astype(F32)
    col_number = lax.broadcasted_iota(jnp.int32, (SPAN, LANES), 0).astype(F32)
    no_terms = jnp.zeros((BAND - 16, LANES), F32)
    no_tail = jnp.zeros((8, LANES), F32)

    for k in range(8 * SCATTER_BATCHES):
        spread[k] = jnp.zeros(((PAD + SPAN + PAD) // 8, 8, LANES), F32)

    for copy in small:
        copy.wait()
    slot = lax.broadcasted_iota(jnp.int32, (1, LANES), 1)
    spare = SLOTS - MOVE_CAP
    places, held = [], []
    for step in range(STEPS):
        place = jnp.full((1, LANES), -1, jnp.int32)
        rank = slot
        for n in range(4 * MOVE_CAP):
            k, m = divmod(n, MOVE_CAP)
            listed = move_slots[4 * step + k, 0, m]
            place = jnp.where(slot == listed, SLOTS * k + m, place)
            rank = rank - jnp.where(slot > listed, 1, 0)
        group = sum(jnp.where(rank >= spare * n, 1, 0) for n in range(1, 4))
        free = jnp.where(
            rank < 4 * spare, (SLOTS - spare) * group + MOVE_CAP + rank, 4 * MOVE_CAP + rank
        )
        place = jnp.where(place < 0, free, place)
        position = lax.broadcasted_iota(jnp.int32, (BLOCKS, LANES), 0)
        held.append(jnp.where(position == place, 1.0, 0.0).astype(BF16))
        places.append(place)

    def by_position(values, n):
        rows = jnp.broadcast_to(values.astype(F32), (8, LANES)).astype(BF16)
        return matmul_t(rows, held[n]).astype(jnp.int32)

    row = lax.broadcasted_iota(jnp.int32, (8, LANES), 0)
    made = jnp.where(row == ORDER_0, by_position(slot, 0), places[1])
    made = jnp.where(row == ORDER_1, by_position(slot, 1), made)
    made = jnp.where(row == SOURCE_1, by_position(places[0], 1), made)
    tables_made[...] = jnp.clip(made, 0, BLOCKS - 1)
    tables_copy = pltpu.make_async_copy(tables_made, tables, table_sem)
    tables_copy.start()

    def strided(ref, first, pitch):
        return [ref[pl.ds(first + i, 8, stride=pitch), :] for i in range(FIELDS)]

    def put_strided(ref, first, pitch, fields):
        for i, x in enumerate(fields):
            ref[pl.ds(first + i, 8, stride=pitch), :] = x

    def slot_of(step, block):
        return block if step == 0 else tables[ORDER_0, block]

    def scatter_one(step, batch, fields, at_spread, bases):
        u, w, v_down, v_cross, s_dd, s_dc, s_cc, mass, volume = fields[:9]
        less = -volume
        values = [mass, mass * v_down, mass * v_cross, less * s_dd, less * s_dc, less * s_cc]
        for k in range(8):
            block = batch * 8 + k
            slot = slot_of(step, block)
            first_row = anchor_down[step, slot] + GHOST
            first_col = anchor_cross[step, slot] + GHOST
            group = lax.shift_right_logical(first_col, 4)
            bases.append(PAD // 8 - 2 * group)
            row_shift = first_row.astype(F32)
            col_shift = (first_col - 16 * group).astype(F32)
            r_value, r_slope = spline_pair(u[k : k + 1] - (row_number - row_shift))
            c_value, c_slope = spline_pair(w[k : k + 1] - (col_number - col_shift))
            c_high, c_low = split(c_value)
            d_high, d_low = split(c_slope)
            rows_kept[block] = jnp.concatenate([r_value, r_slope], axis=0)
            cols_kept[block, :, :LANES] = jnp.concatenate([c_high, c_low], axis=0)
            cols_kept[block, :, LANES:] = jnp.concatenate([d_high, d_low], axis=0)
            m, md, mc, dd, dc, cc = (x[k : k + 1] for x in values)
            first, second = [], []
            for g in range(3):
                r, s = r_value[8 * g : 8 * g + 8], r_slope[8 * g : 8 * g + 8]
                first += [r * m, r * md, r * mc, s * dd, s * dc]
                second += [no_terms, r * dc, r * cc]
            a_high, a_low = split(jnp.concatenate(first + [no_tail], axis=0))
            b_high, b_low = split(jnp.concatenate(second + [no_tail], axis=0))
            left = jnp.concatenate([c_high, c_low, c_high, d_high, d_low, d_high], axis=1)
            a_high, a_low, b_high, b_low = a_high.T, a_low.T, b_high.T, b_low.T
            right = jnp.concatenate([a_high, a_high, a_low, b_high, b_high, b_low], axis=0)
            sums = jnp.dot(left, right, preferred_element_type=F32)
            for v in range(SPAN // 8):
                spread[at_spread + k, PAD // 8 + v] = sums[8 * v : 8 * v + 8]

    def scatter(step, group, fields_of):
        bases = []
        for n in range(SCATTER_BATCHES):
            batch = group * SCATTER_BATCHES + n
            scatter_one(step, batch, fields_of(batch), 8 * n, bases)
        held = [spread[k, pl.ds(base, COLS // 8)] for k, base in enumerate(bases)]
        for v in range(COLS // 8):
            total = grid[step, 8 * v : 8 * v + 8, :]
            for part in held:
                total = total + part[v]
            grid[step, 8 * v : 8 * v + 8, :] = total

    def gather_one(step, batch, source, order, target, pitch, at_stage):
        parts = [[] for _ in range(6)]
        for k in range(8):
            position = batch * 8 + k
            slot = tables[order, position]
            block = slot if step == 0 else tables[SOURCE_1, position]
            group = lax.shift_right_logical(anchor_cross[step, slot] + GHOST, 4)
            cols = cols_kept[block]
            moved = lax.dot_general(
                window[group],
                jnp.concatenate([cols, cols], axis=0),
                (((1,), (0,)), ((), ())),
                preferred_element_type=F32,
            )
            rows = rows_kept[block]
            sums = [None] * 6
            for g in range(3):
                r, s = rows[8 * g : 8 * g + 8], rows[24 + 8 * g : 32 + 8 * g]
                down, cross = moved[16 * g : 16 * g + 8], moved[16 * g + 8 : 16 * g + 16]
                terms = [
                    r * down[:, :LANES],
                    r * cross[:, :LANES],
                    s * down[:, :LANES],
                    s * cross[:, :LANES],
                    r * down[:, LANES:],
                    r * cross[:, LANES:],
                ]
                sums = [t if a is None else a + t for a, t in zip(sums, terms)]
            for held, total in zip(parts, sums):
                held.append(total)
            stage[at_stage + PITCH * k : at_stage + PITCH * k + PITCH, :] = source[block]
        new_down, new_cross, l_dd, l_cd, l_dc, l_cc = (sum_rows(p, sublane) for p in parts)
        f = strided(stage, at_stage, PITCH)
        rate_dc = 0.5 * (l_dc + l_cd)
        trace = l_dd + l_cc
        shear, lame = f[9], f[10]
        updated = [
            jnp.clip(f[0] + TIME_STEP * new_down, 0.5, WIN_DOWN - 1.5),
            jnp.clip(f[1] + TIME_STEP * new_cross, 0.5, WIN_CROSS - 1.5),
            new_down,
            new_cross,
            f[4] + TIME_STEP * (lame * trace + 2.0 * shear * l_dd),
            f[5] + TIME_STEP * (2.0 * shear * rate_dc),
            f[6] + TIME_STEP * (lame * trace + 2.0 * shear * l_cc),
            f[7],
            f[8] * (1.0 + TIME_STEP * trace),
            shear,
            lame,
            f[11] + TIME_STEP * (l_dd * l_dd + l_cc * l_cc + 2.0 * rate_dc * rate_dc),
        ]
        put_strided(target, batch * 8 * pitch, pitch, updated)

    def gather(step, group, source, order, target, pitch):
        for n in range(GATHER_BATCHES):
            batch = group * GATHER_BATCHES + n
            gather_one(step, batch, source, order, target, pitch, 8 * PITCH * n)

    def remote(source, target, send, recv, step):
        return pltpu.make_async_remote_copy(
            src_ref=source,
            dst_ref=target,
            send_sem=send,
            recv_sem=recv,
            device_id=at(step),
            device_id_type=MESH,
        )

    def exchange(step):
        first = grid.at[step, pl.ds(0, 8), :]
        last = grid.at[step, pl.ds(TILE_CROSS, 8), :]
        messages = [
            ((1, 1), last, col_in.at[step, 2]),
            ((-1, 1), last, col_in.at[step, 3]),
            ((1, -1), first, col_in.at[step, 4]),
            ((-1, -1), first, col_in.at[step, 5]),
            ((1, 0), last, col_in.at[step, 6]),
            ((-1, 0), last, col_in.at[step, 7]),
            ((0, 1), last, col_in.at[step, 0]),
            ((0, -1), first, col_in.at[step, 1]),
            ((1, 0), turned.at[step, pl.ds(2 * BAND, BAND), :], band_in.at[step, 0]),
            ((-1, 0), turned.at[step, pl.ds(0, BAND), :], band_in.at[step, 1]),
        ]
        copies = [
            remote(source, target, halo_send.at[step, n], halo_recv.at[step, n], near)
            for n, (near, source, target) in enumerate(messages)
        ]
        for copy in copies[:8]:
            copy.start()
        for t in range(2):
            side = slice(LANES * t, LANES * (t + 1))
            turned[step, :, side] = grid[step, side, :].T[: 3 * BAND]
        for copy in copies[8:]:
            copy.start()
        return copies

    def velocities(step):
        above = me_down > 0
        below = me_down < size_down - 1
        before = me_cross > 0
        after = me_cross < size_cross - 1
        low = lane8 < BAND
        high = (lane8 >= 2 * BAND) & (lane8 < 3 * BAND)
        few = lane8 < 8

        def from_above(there, n):
            return jnp.where(low & above & there, pltpu.roll(col_in[step, n], 48, 1), 0.0)

        def from_below(there, n):
            return jnp.where(high & below & there, pltpu.roll(col_in[step, n], 80, 1), 0.0)

        first = jnp.where(before, col_in[step, 0], 0.0) + from_above(before, 2) + from_below(before, 3)
        last = grid[step, TILE_CROSS : TILE_CROSS + 8, :] + jnp.where(after, col_in[step, 1], 0.0)
        last = last + from_above(after, 4) + from_below(after, 5)
        last = last + from_above(True, 6) + from_below(True, 7)
        edge = jnp.concatenate([first, last, jnp.zeros((LANES - 16, LANES), F32)], axis=0).T

        tiles = []
        for t in range(3):
            col_global = me_cross * TILE_CROSS - GHOST + LANES * t + lane8
            col_keep = (col_global > 0) & (col_global < TILE_CROSS * size_cross - 1)
            side = slice(LANES * t, LANES * (t + 1))
            found = []
            for g in range(3):
                row_global = me_down * TILE_DOWN - GHOST + 8 * g + sublane
                inside = col_keep & (row_global > 0) & (row_global < TILE_DOWN * size_down - 1)
                sums = []
                for channel in range(5):
                    here = slice(BAND * g + 8 * channel, BAND * g + 8 * channel + 8)
                    if t == 2:
                        sums.append(jnp.where(few, pltpu.roll(edge[here], LANES - 8, 1), 0.0))
                        continue
                    total = turned[step, here, side]
                    there = slice(8 * channel, 8 * channel + 8)
                    if g == 0:
                        total = total + jnp.where(above, band_in[step, 0, there, side], 0.0)
                    if g == 2:
                        total = total + jnp.where(below, band_in[step, 1, there, side], 0.0)
                    if t == 0:
                        total = total + jnp.where(few, edge[here], 0.0)
                    sums.append(total)
                mass, moved_down, moved_cross, force_down, force_cross = sums
                heavy = jnp.maximum(mass, MASS_FLOOR)
                v_down = (moved_down + TIME_STEP * (force_down + GRAVITY * mass)) / heavy
                v_cross = (moved_cross + TIME_STEP * force_cross) / heavy
                found += [jnp.where(inside, v_down, 0.0), jnp.where(inside, v_cross, 0.0)]
            tiles.append(jnp.concatenate(found, axis=0))
        tops = [x.astype(BF16).astype(F32) for x in tiles]
        rests = [x - top for x, top in zip(tiles, tops)]
        lane48 = lax.broadcasted_iota(jnp.int32, (48, LANES), 1)

        def turn(x, m):
            return pltpu.roll(x, 16 * m, 1) if m else x

        def side_by_side(a, b, c, d):
            return jnp.where(
                lane48 < 64,
                jnp.where(lane48 < 32, a, b),
                jnp.where(lane48 < 96, c, d),
            ).astype(BF16)

        for t in range(2):
            high_turned = [turn(tops[t], m) for m in range(8)]
            low_turned = [turn(rests[t], m) for m in range(8)]
            for q in range(7):
                window[8 * t + q] = side_by_side(
                    high_turned[(8 - q) % 8],
                    high_turned[(10 - q) % 8],
                    low_turned[(12 - q) % 8],
                    low_turned[(14 - q) % 8],
                )
            a = jnp.where(lane48 < 16, tops[t + 1], tops[t])
            b = jnp.where(lane48 < 16, rests[t + 1], rests[t])
            window[8 * t + 7] = side_by_side(turn(a, 1), turn(a, 3), turn(b, 5), turn(b, 7))

    def wait_all(copies):
        for copy in copies:
            copy.wait()

    def send_blocks(step, first):
        copies = []
        for k in (first, first + 1):
            near = MOVES[k]
            copy = remote(
                leaving.at[step, pl.ds(k * SLOTS * FIELDS, SEND_ROWS), :],
                arrived.at[step, pl.ds((k ^ 1) * SLOTS * FIELDS, SEND_ROWS), :],
                move_send.at[step, k],
                move_recv.at[step, k],
                near,
            )
            copy.start()
            copies.append(copy)
        return copies

    for step in range(STEPS):
        grid[step] = jnp.zeros((COLS, LANES), F32)

    def fields_0(batch):
        rows = pl.ds(pl.multiple_of(batch * 8, 8), 8)
        fields = [fields_in[i, rows, :] for i in range(FIELDS)]
        put_strided(flat_0, batch * 8 * PITCH, PITCH, fields)
        return fields

    def scatter_0(group, carry):
        scatter(0, group, fields_0)
        return carry

    batches = BLOCKS // 8 // SCATTER_BATCHES
    for n, load in enumerate(loads):
        load.wait()
        lax.fori_loop(n * batches // LOADS, (n + 1) * batches // LOADS, scatter_0, 0)
    tables_copy.wait()
    pl.semaphore_wait(barrier, len(NEAR))
    wait_all(exchange(0))
    velocities(0)

    def gather_leaving_0(batch, carry):
        gather(0, batch, state_0, ORDER_0, leaving.at[0], FIELDS)
        return carry

    def gather_staying_0(batch, carry):
        gather(0, batch, state_0, ORDER_0, flat_1, PITCH)
        return carry

    lax.fori_loop(0, 1, gather_leaving_0, 0)
    copies = send_blocks(0, 0)
    lax.fori_loop(1, 2, gather_leaving_0, 0)
    copies += send_blocks(0, 2)
    lax.fori_loop(2, 4, gather_staying_0, 0)

    def settled(step, batch):
        here = (lax.rem(batch, 2) * 8 + sublane) < count[step, batch // 2]
        first = batch * 8 * FIELDS
        came = strided(arrived.at[step], first, FIELDS)
        kept = strided(leaving.at[step], first, FIELDS)
        return [jnp.where(here, a, b) for a, b in zip(came, kept)]

    def fields_staying(batch):
        return strided(flat_1, batch * 8 * PITCH, PITCH)

    def fields_arrived(batch):
        fields = settled(0, batch)
        put_strided(flat_1, batch * 8 * PITCH, PITCH, fields)
        return fields

    def scatter_staying(group, carry):
        scatter(1, group, fields_staying)
        return carry

    def scatter_arrived(group, carry):
        scatter(1, group, fields_arrived)
        return carry

    lax.fori_loop(2, 4, scatter_staying, 0)
    wait_all(copies)
    lax.fori_loop(0, 2, scatter_arrived, 0)
    wait_all(exchange(1))
    velocities(1)

    def gather_leaving_1(batch, carry):
        gather(1, batch, state_1, ORDER_1, leaving.at[1], FIELDS)
        return carry

    def gather_staying_1(batch, carry):
        gather(1, batch, state_1, ORDER_1, flat_2, PITCH)
        return carry

    lax.fori_loop(0, 1, gather_leaving_1, 0)
    copies = send_blocks(1, 0)
    lax.fori_loop(1, 2, gather_leaving_1, 0)
    copies += send_blocks(1, 2)
    lax.fori_loop(2, 4, gather_staying_1, 0)
    wait_all(copies)

    def settle(group, carry):
        for n in range(4):
            batch = 4 * group + n
            put_strided(flat_2, batch * 8 * PITCH, PITCH, settled(1, batch))
        return carry

    lax.fori_loop(0, 2, settle, 0)

    def put(group, carry):
        for k in range(8 * GATHER_BATCHES):
            place = tables[PLACE_1, group * 8 * GATHER_BATCHES + k]
            stage[PITCH * k : PITCH * k + PITCH, :] = state_2[place]
        for n in range(GATHER_BATCHES):
            rows = pl.ds(pl.multiple_of((group * GATHER_BATCHES + n) * 8, 8), 8)
            for i, x in enumerate(strided(stage, 8 * PITCH * n, PITCH)):
                result[i, rows, :] = x
        return carry

    lax.fori_loop(0, BLOCKS // 8 // GATHER_BATCHES, put, 0)


def on_device(particles, anchor_down, anchor_cross, move_count, move_slots):
    vmem = pl.BlockSpec(memory_space=pltpu.VMEM)
    by_field = pl.pallas_call(
        kernel,
        out_shape=jax.ShapeDtypeStruct((FIELDS, BLOCKS, LANES), F32),
        in_specs=[pl.BlockSpec(memory_space=pltpu.HBM)] * 5,
        out_specs=vmem,
        scratch_shapes=[
            pltpu.VMEM((FIELDS, BLOCKS, LANES), F32),
            pltpu.VMEM((8 * PITCH * GATHER_BATCHES + STRIDE_PAD, LANES), F32),
            pltpu.VMEM((BLOCKS, 48, LANES), F32),
            pltpu.VMEM((BLOCKS, 2 * SPAN, 2 * LANES), BF16),
            pltpu.VMEM((8 * SCATTER_BATCHES, (PAD + SPAN + PAD) // 8, 8, LANES), F32),
            pltpu.VMEM((STEPS, COLS, LANES), F32),
            pltpu.VMEM((STEPS, 3 * BAND, 2 * LANES), F32),
            pltpu.VMEM((STEPS, 2, BAND, 2 * LANES), F32),
            pltpu.VMEM((STEPS, 8, 8, LANES), F32),
            pltpu.VMEM((16, 48, LANES), BF16),
            pltpu.VMEM((STEPS, OUT_ROWS + STRIDE_PAD, LANES), F32),
            pltpu.VMEM((STEPS, OUT_ROWS + STRIDE_PAD, LANES), F32),
            pltpu.VMEM((BLOCKS + 1, PITCH, LANES), F32),
            pltpu.VMEM((BLOCKS + 1, PITCH, LANES), F32),
            pltpu.VMEM((BLOCKS + 1, PITCH, LANES), F32),
            pltpu.SemaphoreType.DMA((STEPS, 10)),
            pltpu.SemaphoreType.DMA((STEPS, 10)),
            pltpu.SemaphoreType.DMA((STEPS, 4)),
            pltpu.SemaphoreType.DMA((STEPS, 4)),
            pltpu.SemaphoreType.DMA((LOADS,)),
            pltpu.VMEM((8, LANES), jnp.int32),
            pltpu.SMEM((8, LANES), jnp.int32),
            pltpu.SemaphoreType.DMA,
            pltpu.SMEM((STEPS * 4, 1, MOVE_CAP), jnp.int32),
            pltpu.SMEM((STEPS, BLOCKS), jnp.int32),
            pltpu.SMEM((STEPS, BLOCKS), jnp.int32),
            pltpu.SMEM((STEPS, 4), jnp.int32),
            pltpu.SemaphoreType.DMA((4,)),
        ],
        compiler_params=pltpu.CompilerParams(
            collective_id=0, has_side_effects=True, vmem_limit_bytes=40 * 1024 * 1024
        ),
    )(
        *(
            pltpu.with_memory_space_constraint(x, pltpu.HBM)
            for x in (
                move_slots.reshape(STEPS * 4, 1, MOVE_CAP),
                anchor_down,
                anchor_cross,
                move_count[:, :, 0, 0],
                jnp.transpose(particles, (1, 0, 2)),
            )
        )
    )
    return jnp.transpose(by_field, (1, 0, 2))


def solution(mesh):
    return jax.shard_map(
        on_device,
        mesh=mesh,
        in_specs=(
            P(("down", "cross"), None, None),
            P(None, ("down", "cross")),
            P(None, ("down", "cross")),
            P(None, None, "down", "cross"),
            P(None, None, None, "down", "cross"),
        ),
        out_specs=P(("down", "cross"), None, None),
        check_vma=False,
    )
```
